128 devices in a mesh: chan: 32 (over z, x, core), bl: 4 (over y).
Axes of the slice: x: 4, y: 4, z: 4, core: 2. Of those that a mesh axis runs over, the one named last changes fastest.
Arguments:
- visibilities: bfloat16 [1024, 1536, 2, 128], P('bl', 'chan'), may hold values from -6 to 6
- kernels: bfloat16 [64, 128, 256], replicated, may hold values from -0.1875 to 0.1875
- block_ids: int32 [4, 256, 8], P('bl'), may hold values from 0 to 255
- kernel_ids: int32 [4, 256, 8], P('bl'), may hold values from 0 to 63
- tile_counts: int32 [4, 256], P('bl'), may hold values from 1 to 8, as said below
- wedge_mask: int32 [256, 1536], P(('chan', 'bl')), may hold values 0 or 1
Outputs:
- delay_tiles: float32 [256, 2, 256, 1536], P(('chan', 'bl'))
The draws below stay inside these ranges and needn't reach their ends.
Inputs may be any that keep to these rules, and one draw needn't show every extreme that they name: `tile_counts`: slots at or past a tile's count are ignored; in every group some tile uses all 8 slots.
All inputs are finite; a program needn't handle non-finite values. No bound on the sum of `wedge_mask` on one device may be relied on, other than what follows from the above.
Results may differ from the reference program's by a relative error of at most 0.0095.
Values may be sent and summed in bfloat16 or wider, within the bound.
A program may use at most 128 MiB of HBM per device.

```python
import math
import jax
import jax.numpy as jnp
from jax import lax

NCH = 1536
CELLS = 256
SB = 128
MOST = 8
NK = 64
NB = 256
TILES = 256
N_BL = 4


def draw_tile_counts(key, part):
    counts = jax.random.randint(key, (N_BL, TILES), 1, MOST + 1, dtype=jnp.int32)
    return counts.at[:, 0].set(MOST)


def with_ends(result, stream_key, least, top_value):
    place = [jax.random.randint(jax.random.fold_in(stream_key, axis), (), 0, length) for axis, length in enumerate(result.shape)]
    longest = result.shape.index(max(result.shape))
    neighbour = place[:longest] + [(place[longest] + 1) % result.shape[longest]] + place[longest + 1:]
    return result.at[tuple(place)].set(least).at[tuple(neighbour)].set(top_value)


def level_of(stream_key, shape, pieces, low, top_value):
    def one(position, blocks):
        heights = jax.random.uniform(jax.random.fold_in(jax.random.fold_in(stream_key, 6), position), (blocks,), jnp.float32, low / len(pieces), top_value / len(pieces))
        return jnp.repeat(jnp.exp(heights), shape[position] // blocks).reshape((-1,) + (1,) * (len(shape) - position - 1))

    loudness = one(*pieces[0])
    for cut in pieces[1:]:
        loudness = loudness * one(*cut)
    return loudness


def noise(key, dims, scale, reach, shards=(), held_as=jnp.bfloat16):
    level = level_of(key, dims, shards, -0.22, 0.18) if shards else 1.0
    array = jax.random.normal(key, dims, jnp.float32) * scale * level
    return jnp.minimum(jnp.maximum(array, -reach), reach).astype(held_as)


def setup_inputs(seed: int = 0) -> dict:
    key_of = jax.random.split(jax.random.key(seed), 7)
    visibilities = noise(key_of[0], (N_BL * NB, NCH, 2, SB), 1.0, 6.0, ((0, 4), (1, 32)))
    kernels = noise(key_of[1], (NK, SB, CELLS), (SB * MOST) ** -0.5, 0.1875)
    block_ids = with_ends(jax.random.randint(key_of[2], (N_BL, TILES, MOST), 0, NB), jax.random.fold_in(key_of[2], 1), 0, NB - 1).astype(jnp.int32)
    kernel_ids = with_ends(jax.random.randint(key_of[3], (N_BL, TILES, MOST), 0, NK), jax.random.fold_in(key_of[3], 1), 0, NK - 1).astype(jnp.int32)
    tile_counts = draw_tile_counts(jax.random.fold_in(key_of[6], 71), 0)
    wedge_mask = with_ends((jax.random.randint(key_of[5], (TILES, NCH), 0, 2) < 1).astype(jnp.int32), jax.random.fold_in(key_of[5], 1), 0, 1)
    return {"visibilities": visibilities, "kernels": kernels, "block_ids": block_ids, "kernel_ids": kernel_ids, "tile_counts": tile_counts, "wedge_mask": wedge_mask}


def delay_tables():
    chans = jnp.arange(NCH, dtype=jnp.int32)
    phase = chans[:, None] * chans[None, :] % NCH
    angle = phase.astype(jnp.float32) * (2.0 * math.pi / NCH)
    return (jnp.cos(angle).astype(jnp.bfloat16), jnp.sin(angle).astype(jnp.bfloat16))

def reference(visibilities, kernels, block_ids, kernel_ids, tile_counts, wedge_mask):
    blocked = visibilities.reshape(N_BL, NB, NCH, 2, SB)
    cosine, sine = delay_tables()
    slots = jnp.arange(MOST, dtype=jnp.int32)
    scale = 1.0 / math.sqrt(NCH)

    def one_tile(tile):
        total = jnp.zeros((NCH, 2, CELLS), jnp.float32)
        for group in range(N_BL):
            chosen = blocked[group][block_ids[group, tile]]
            keep = (slots < tile_counts[group, tile]).astype(jnp.bfloat16)
            weights = kernels[kernel_ids[group, tile]] * keep[:, None, None]
            part = jnp.einsum('kcps,ksx->cpx', chosen.astype(jnp.float32), weights.astype(jnp.float32))
            rounded = lax.optimization_barrier(part.astype(jnp.bfloat16))
            total = total + rounded.astype(jnp.float32)
        gridded = total.astype(jnp.bfloat16)
        real_part = gridded[:, 0].T
        imag_part = gridded[:, 1].T
        out_real = jnp.dot(real_part, cosine, preferred_element_type=jnp.float32) + jnp.dot(imag_part, sine, preferred_element_type=jnp.float32)
        out_imag = jnp.dot(imag_part, cosine, preferred_element_type=jnp.float32) - jnp.dot(real_part, sine, preferred_element_type=jnp.float32)
        keep_bins = wedge_mask[tile].astype(jnp.float32)
        return jnp.stack([out_real, out_imag]) * scale * keep_bins[None, None, :]
    return lax.map(one_tile, jnp.arange(TILES, dtype=jnp.int32))
```

```python
import functools
import math

import jax
import jax.numpy as jnp
import ml_dtypes
import numpy as np
from jax import lax
from jax.experimental import pallas as pl
from jax.experimental.pallas import tpu as pltpu
from jax.sharding import PartitionSpec as P

MESH = pl.DeviceIdType.MESH
STAGES = 16
PER = 4


def tables(nchan):
    chans = np.arange(nchan, dtype=np.int64)
    phase = chans[:, None] * chans[None, :] % nchan
    angle = phase.astype(np.float32) * np.float32(2.0 * math.pi / nchan)
    cosine, sine = np.cos(angle), np.sin(angle)
    real = np.stack([cosine, sine], axis=1).reshape(2 * nchan, nchan)
    imag = np.stack([-sine, cosine], axis=1).reshape(2 * nchan, nchan)
    return real.astype(ml_dtypes.bfloat16), imag.astype(ml_dtypes.bfloat16)


def grid_kernel(
    n_chan, n_bl, bid, kid, cnt, vis_hbm, ker_hbm, grid_out,
    vis, ker, opp, to_right, to_left, opp_in_a, opp_in_b, from_left, from_right, own,
    load_sem, opp_s, opp_r, nbr_s, nbr_r, own_s, own_r,
):
    chan = lax.axis_index("chan")
    y = lax.axis_index("bl")
    right, left = lax.rem(y + 1, n_bl), lax.rem(y + n_bl - 1, n_bl)
    far = lax.rem(y + 2, n_bl)
    blocks = vis.shape[0]
    kinds = ker_hbm.shape[0]
    cut = blocks // 4
    loads = [
        pltpu.make_async_copy(
            vis_hbm.at[pl.ds(q * cut, cut)], vis.at[pl.ds(q * cut, cut)], load_sem.at[q]
        )
        for q in range(4)
    ] + [
        pltpu.make_async_copy(
            ker_hbm.at[pl.ds(q * 32, 32)], ker.at[pl.ds(q * 32, 32)], load_sem.at[4 + q]
        )
        for q in range(2)
    ]
    for one in loads:
        one.start()
    ker[kinds] = jnp.zeros(ker.shape[1:], ker.dtype)

    barrier = pltpu.get_barrier_semaphore()

    def greet(o, carry):
        pl.semaphore_signal(
            barrier, inc=1, device_id=(lax.rem(chan + o, n_chan), y), device_id_type=MESH
        )
        return carry

    lax.fori_loop(1, n_chan, greet, 0)
    for other in (left, right):
        pl.semaphore_signal(barrier, inc=1, device_id=(chan, other), device_id_type=MESH)
    pl.semaphore_wait(barrier, n_chan + 1)
    for one in loads:
        one.wait()

    core = lax.rem(chan, 2)
    col = lax.rem(lax.div(chan, 2), 4)
    row = lax.div(chan, 8)

    def owner(s, e):
        m = STAGES - 1 - s
        dz = lax.rem(m, 4)
        dx = lax.rem(lax.div(m, 4) + m, 4)
        return (lax.rem(row + dz, 4) * 4 + lax.rem(col + dx, 4)) * 2 + lax.rem(core + e, 2)

    def partial(tile):
        count = cnt[0, tile]
        left_side, right_side = [], []
        for k in range(8):
            b = bid[tile, k]
            q = jnp.where(k < count, kid[tile, k], kinds)
            left_side.append(vis[b])
            right_side.append(ker[q])
        return jnp.dot(
            jnp.concatenate(left_side, axis=1),
            jnp.concatenate(right_side, axis=0),
            preferred_element_type=jnp.float32,
        )

    def tile_of(s, j, plane):
        return (owner(s, lax.div(j, 2)) * n_bl + plane) * 2 + lax.rem(j, 2)

    def remote(src, dst, send, recv, plane):
        return pltpu.make_async_remote_copy(
            src_ref=src, dst_ref=dst, send_sem=send, recv_sem=recv,
            device_id=(chan, plane), device_id_type=MESH,
        )

    def opp_copies(s):
        return (
            remote(opp.at[s, pl.ds(0, 2)], opp_in_a.at[s], opp_s.at[0, s], opp_r.at[0, s], left),
            remote(opp.at[s, pl.ds(2, 2)], opp_in_b.at[s], opp_s.at[1, s], opp_r.at[1, s], right),
        )

    def nbr_copies(s):
        return (
            remote(to_left.at[s], from_right.at[s], nbr_s.at[0, s], nbr_r.at[0, s], left),
            remote(to_right.at[s], from_left.at[s], nbr_s.at[1, s], nbr_r.at[1, s], right),
        )

    def own_copy(s, e):
        return pltpu.make_async_remote_copy(
            src_ref=own.at[s, pl.ds(2 * e, 2)],
            dst_ref=grid_out.at[:, chan],
            send_sem=own_s.at[s, e], recv_sem=own_r.at[s, e],
            device_id=(owner(s, e), y), device_id_type=MESH,
        )

    def self_copy():
        return pltpu.make_async_copy(
            own.at[STAGES - 1, pl.ds(0, 2)], grid_out.at[:, chan], own_r.at[STAGES - 1, 0]
        )

    def step(it, carry):
        @pl.when(it < STAGES)
        def _():
            s = it

            def one(j, c):
                opp[s, j] = partial(tile_of(s, j, far)).astype(jnp.bfloat16)
                return c

            lax.fori_loop(0, PER, one, 0)
            for copy in opp_copies(s):
                copy.start()

        @pl.when((it >= 1) & (it < STAGES + 1))
        def _():
            s = it - 1
            for copy in opp_copies(s):
                copy.wait_recv()
            go_left, go_right = nbr_copies(s)

            def plain(j, c):
                to_right[s, j] = partial(tile_of(s, j, right)).astype(jnp.bfloat16)
                to_left[s, j + 2] = partial(tile_of(s, j + 2, left)).astype(jnp.bfloat16)
                return c

            def added(j, c):
                to_right[s, j + 2] = (
                    partial(tile_of(s, j + 2, right)) + opp_in_b[s, j].astype(jnp.float32)
                ).astype(jnp.bfloat16)
                to_left[s, j] = (
                    partial(tile_of(s, j, left)) + opp_in_a[s, j].astype(jnp.float32)
                ).astype(jnp.bfloat16)
                return c

            lax.fori_loop(0, 2, plain, 0)
            lax.fori_loop(0, 2, added, 0)
            go_left.start()
            go_right.start()

        @pl.when(it >= 2)
        def _():
            s = it - 2
            for copy in nbr_copies(s):
                copy.wait_recv()

            def one(j, c):
                total = partial(tile_of(s, j, y))
                total += from_left[s, j].astype(jnp.float32)
                total += from_right[s, j].astype(jnp.float32)
                own[s, j] = total.astype(jnp.bfloat16)
                return c

            lax.fori_loop(0, PER, one, 0)

            @pl.when(s < STAGES - 1)
            def _():
                own_copy(s, 0).start()

            own_copy(s, 1).start()

            @pl.when(s == STAGES - 1)
            def _():
                self_copy().start()

        return carry

    lax.fori_loop(0, STAGES + 2, step, 0)

    def drain(s, carry):
        for copy in opp_copies(s):
            copy.wait_send()
        for copy in nbr_copies(s):
            copy.wait_send()

        @pl.when(s < STAGES - 1)
        def _():
            own_copy(s, 0).wait()

        own_copy(s, 1).wait()
        return carry

    lax.fori_loop(0, STAGES, drain, 0)
    self_copy().wait()


def local(n_chan, n_bl, real_table, imag_table, visibilities, kernels, block_ids, kernel_ids, tile_counts, wedge_mask):
    blocks, ch_dev = visibilities.shape[:2]
    length, cells = kernels.shape[1:]
    rows = ch_dev * 2
    bf16 = jnp.bfloat16
    stage = (STAGES, PER, rows, cells)
    half = (STAGES, PER // 2, rows, cells)
    any_space = pl.BlockSpec(memory_space=pl.ANY)
    smem = pl.BlockSpec(memory_space=pltpu.SMEM)
    grids = pl.pallas_call(
        functools.partial(grid_kernel, n_chan, n_bl),
        out_shape=jax.ShapeDtypeStruct((2, n_chan, rows, cells), bf16),
        in_specs=[smem, smem, smem, any_space, any_space],
        out_specs=any_space,
        scratch_shapes=[
            pltpu.VMEM((blocks, rows, length), bf16),
            pltpu.VMEM((kernels.shape[0] + 1, length, cells), bf16),
            pltpu.VMEM(stage, bf16),
            pltpu.VMEM(stage, bf16),
            pltpu.VMEM(stage, bf16),
            pltpu.VMEM(half, bf16),
            pltpu.VMEM(half, bf16),
            pltpu.VMEM(stage, bf16),
            pltpu.VMEM(stage, bf16),
            pltpu.VMEM(stage, bf16),
            pltpu.SemaphoreType.DMA((6,)),
            pltpu.SemaphoreType.DMA((2, STAGES)),
            pltpu.SemaphoreType.DMA((2, STAGES)),
            pltpu.SemaphoreType.DMA((2, STAGES)),
            pltpu.SemaphoreType.DMA((2, STAGES)),
            pltpu.SemaphoreType.DMA((STAGES, 2)),
            pltpu.SemaphoreType.DMA((STAGES, 2)),
        ],
        compiler_params=pltpu.CompilerParams(
            collective_id=0, has_side_effects=True, vmem_limit_bytes=44 << 20
        ),
        name="grid_exchange",
    )(
        block_ids[0], kernel_ids[0], tile_counts,
        visibilities.reshape(blocks, rows, length), kernels,
    )
    nchan = n_chan * ch_dev
    gridded = grids.reshape(2, 2 * nchan, cells)
    keep = wedge_mask.astype(jnp.float32)[:, None, None, :]
    scale = 1.0 / math.sqrt(nchan)
    out_real = jnp.einsum("tkx,kd->txd", gridded, real_table, preferred_element_type=jnp.float32)
    out_imag = jnp.einsum("tkx,kd->txd", gridded, imag_table, preferred_element_type=jnp.float32)
    return jnp.stack([out_real, out_imag], axis=1) * scale * keep


def solution(mesh):
    def run(visibilities, *rest):
        real_table, imag_table = tables(visibilities.shape[1])
        return jax.shard_map(
            functools.partial(
                local, mesh.shape["chan"], mesh.shape["bl"],
                jnp.asarray(real_table), jnp.asarray(imag_table),
            ),
            mesh=mesh,
            in_specs=(
                P("bl", "chan", None, None),
                P(),
                P("bl", None, None),
                P("bl", None, None),
                P("bl", None),
                P(("chan", "bl"), None),
            ),
            out_specs=P(("chan", "bl"), None, None, None),
            check_vma=False,
        )(visibilities, *rest)

    return run
```

```python
import functools
import math

import jax
import jax.numpy as jnp
import ml_dtypes
import numpy as np
from jax import lax
from jax.experimental import pallas as pl
from jax.experimental.pallas import tpu as pltpu
from jax.sharding import PartitionSpec as P

MESH = pl.DeviceIdType.MESH
STAGES = 16
PER = 4


def tables(nchan, ch_dev):
    half = nchan // 2
    delays = np.arange(half, dtype=np.int64)
    result = []
    for odd in range(2):
        chans = np.arange(nchan, dtype=np.int64).reshape(nchan // ch_dev, ch_dev)[:, odd::2]
        phase = chans[:, :, None] * delays % nchan
        angle = phase.astype(np.float32) * np.float32(2.0 * math.pi / nchan)
        cosine, sine = np.cos(angle), np.sin(angle)
        real = np.stack([cosine, sine], axis=1)
        imag = np.stack([-sine, cosine], axis=1)
        both = np.concatenate([real, imag], axis=3).reshape(nchan, nchan)
        result.append(both.astype(ml_dtypes.bfloat16))
    return np.stack(result)


def grid_kernel(
    n_chan, n_bl, bid_hbm, kid_hbm, cnt_hbm, vis_hbm, ker_hbm, grid_out,
    bid, kid, cnt, vis, ker, sums, opp, to_right, to_left, opp_in_a, opp_in_b, from_left, from_right, own,
    load_sem, opp_s, opp_r, nbr_s, nbr_r, own_s, own_r,
):
    chan = lax.axis_index("chan")
    y = lax.axis_index("bl")
    right, left = lax.rem(y + 1, n_bl), lax.rem(y + n_bl - 1, n_bl)
    far = lax.rem(y + 2, n_bl)
    blocks = vis.shape[0]
    kinds = ker_hbm.shape[0]
    cut = blocks // 4
    rows = vis.shape[1]
    loads = [
        pltpu.make_async_copy(
            vis_hbm.at[pl.ds(q * cut, cut)], vis.at[pl.ds(q * cut, cut)], load_sem.at[q]
        )
        for q in range(4)
    ] + [
        pltpu.make_async_copy(
            ker_hbm.at[pl.ds(q * 32, 32)], ker.at[pl.ds(q * 32, 32)], load_sem.at[4 + q]
        )
        for q in range(2)
    ] + [
        pltpu.make_async_copy(src, dst, load_sem.at[6 + q])
        for q, (src, dst) in enumerate(((bid_hbm, bid), (kid_hbm, kid), (cnt_hbm, cnt)))
    ]
    for one in loads:
        one.start()
    ker[kinds] = jnp.zeros(ker.shape[1:], ker.dtype)

    barrier = pltpu.get_barrier_semaphore()

    def greet(o, carry):
        pl.semaphore_signal(
            barrier, inc=1, device_id=(lax.rem(chan + o, n_chan), y), device_id_type=MESH
        )
        return carry

    lax.fori_loop(1, n_chan, greet, 0)
    for other in (left, right):
        pl.semaphore_signal(barrier, inc=1, device_id=(chan, other), device_id_type=MESH)
    pl.semaphore_wait(barrier, n_chan + 1)
    for one in loads:
        one.wait()

    core = lax.rem(chan, 2)
    col = lax.rem(lax.div(chan, 2), 4)
    row = lax.div(chan, 8)

    def owner(s, e):
        m = STAGES - 1 - s
        dz = lax.rem(m, 4)
        dx = lax.rem(lax.div(m, 4) + m, 4)
        return (lax.rem(row + dz, 4) * 4 + lax.rem(col + dx, 4)) * 2 + lax.rem(core + e, 2)

    def partial(tile):
        count = cnt[0, tile]
        left_side, right_side = [], []
        for k in range(8):
            b = bid[k, tile]
            q = jnp.where(k < count, kid[k, tile], kinds)
            left_side.append(vis[b])
            right_side.append(ker[q])
        return jnp.dot(
            jnp.concatenate(left_side, axis=1),
            jnp.concatenate(right_side, axis=0),
            preferred_element_type=jnp.float32,
        )

    def tile_of(s, j, plane):
        return (owner(s, j // 2) * n_bl + plane) * 2 + j % 2

    def remote(src, dst, send, recv, plane):
        return pltpu.make_async_remote_copy(
            src_ref=src, dst_ref=dst, send_sem=send, recv_sem=recv,
            device_id=(chan, plane), device_id_type=MESH,
        )

    def opp_copies(s):
        return (
            remote(opp.at[s, pl.ds(0, 2)], opp_in_a.at[s], opp_s.at[0, s], opp_r.at[0, s], left),
            remote(opp.at[s, pl.ds(2, 2)], opp_in_b.at[s], opp_s.at[1, s], opp_r.at[1, s], right),
        )

    def nbr_copies(s):
        return (
            remote(to_left.at[s], from_right.at[s], nbr_s.at[0, s], nbr_r.at[0, s], left),
            remote(to_right.at[s], from_left.at[s], nbr_s.at[1, s], nbr_r.at[1, s], right),
        )

    def own_copy(s, e):
        return pltpu.make_async_remote_copy(
            src_ref=own.at[s, pl.ds(2 * e, 2)],
            dst_ref=grid_out.at[:, :, chan],
            send_sem=own_s.at[s, e], recv_sem=own_r.at[s, e],
            device_id=(owner(s, e), y), device_id_type=MESH,
        )

    def self_copy():
        return pltpu.make_async_copy(
            own.at[STAGES - 1, pl.ds(0, 2)], grid_out.at[:, :, chan], own_r.at[STAGES - 1, 0]
        )

    def step(it, carry):
        @pl.when(it < STAGES)
        def _():
            s = it

            for j in range(PER):
                opp[s, j] = partial(tile_of(s, j, far)).astype(jnp.bfloat16)
            for copy in opp_copies(s):
                copy.start()

        @pl.when((it >= 1) & (it < STAGES + 1))
        def _():
            s = it - 1
            for copy in opp_copies(s):
                copy.wait_recv()
            go_left, go_right = nbr_copies(s)

            for j in range(2):
                to_right[s, j] = partial(tile_of(s, j, right)).astype(jnp.bfloat16)
                to_left[s, j + 2] = partial(tile_of(s, j + 2, left)).astype(jnp.bfloat16)
            for j in range(2):
                to_right[s, j + 2] = (
                    partial(tile_of(s, j + 2, right)) + opp_in_b[s, j].astype(jnp.float32)
                ).astype(jnp.bfloat16)
                to_left[s, j] = (
                    partial(tile_of(s, j, left)) + opp_in_a[s, j].astype(jnp.float32)
                ).astype(jnp.bfloat16)
            go_left.start()
            go_right.start()

        @pl.when(it >= 2)
        def _():
            s = it - 2
            for copy in nbr_copies(s):
                copy.wait_recv()

            for j in range(PER):
                total = partial(tile_of(s, j, y))
                total += from_left[s, j].astype(jnp.float32)
                total += from_right[s, j].astype(jnp.float32)
                for lane in range(sums.shape[1]):
                    sums[j, lane] = total[:, lane * 128 : lane * 128 + 128]
                for odd in range(2):
                    sorted_rows = [
                        jnp.concatenate(
                            [sums[j, lane, pl.ds(2 * odd + p, rows // 4, stride=4)] for p in range(2)],
                            axis=0,
                        )
                        for lane in range(sums.shape[1])
                    ]
                    own[s, j, odd] = jnp.concatenate(sorted_rows, axis=1).astype(jnp.bfloat16)

            @pl.when(s < STAGES - 1)
            def _():
                own_copy(s, 0).start()

            own_copy(s, 1).start()

            @pl.when(s == STAGES - 1)
            def _():
                self_copy().start()

        return carry

    lax.fori_loop(0, STAGES + 2, step, 0)

    def drain(s, carry):
        for copy in opp_copies(s):
            copy.wait_send()
        for copy in nbr_copies(s):
            copy.wait_send()

        @pl.when(s < STAGES - 1)
        def _():
            own_copy(s, 0).wait()

        own_copy(s, 1).wait()
        return carry

    lax.fori_loop(0, STAGES, drain, 0)
    self_copy().wait()


def delay_kernel(grids, table, keep, out_hbm, left, out, sem):
    tiles, parities, nchan, cells = grids.shape
    half = nchan // 2
    width = cells
    scale = 1.0 / math.sqrt(nchan)
    copies = []
    for t in range(tiles):
        for odd in range(parities):
            left[t, odd] = grids[t, odd].T
        for part in range(2):
            for q in range(half // width):
                at = part * half + q * width
                even_sum, odd_sum = (
                    jnp.dot(
                        left[t, odd], table[odd, :, at : at + width],
                        preferred_element_type=jnp.float32,
                    )
                    for odd in range(2)
                )
                for side, value in enumerate((even_sum + odd_sum, even_sum - odd_sum)):
                    lane = side * half + q * width
                    bins = keep[t : t + 1, lane : lane + width].astype(jnp.float32) * scale
                    out[t, part, :, lane : lane + width] = value * bins
                    copy = pltpu.make_async_copy(
                        out.at[t, part, :, pl.ds(lane, width)],
                        out_hbm.at[t, part, :, pl.ds(lane, width)],
                        sem.at[len(copies)],
                    )
                    copy.start()
                    copies.append(copy)
    for copy in copies:
        copy.wait()


def local(n_chan, n_bl, table, visibilities, kernels, block_ids, kernel_ids, tile_counts, wedge_mask):
    blocks, ch_dev = visibilities.shape[:2]
    length, cells = kernels.shape[1:]
    rows = ch_dev * 2
    bf16 = jnp.bfloat16
    stage = (STAGES, PER, rows, cells)
    half = (STAGES, PER // 2, rows, cells)
    any_space = pl.BlockSpec(memory_space=pl.ANY)
    hbm = pl.BlockSpec(memory_space=pltpu.HBM)
    grids = pl.pallas_call(
        functools.partial(grid_kernel, n_chan, n_bl),
        out_shape=jax.ShapeDtypeStruct((2, 2, n_chan, rows // 2, cells), bf16),
        in_specs=[hbm] * 5,
        out_specs=any_space,
        scratch_shapes=[
            pltpu.SMEM(block_ids.shape[:0:-1], jnp.int32),
            pltpu.SMEM(block_ids.shape[:0:-1], jnp.int32),
            pltpu.SMEM(tile_counts.shape, jnp.int32),
            pltpu.VMEM((blocks, rows, length), bf16),
            pltpu.VMEM((kernels.shape[0] + 1, length, cells), bf16),
            pltpu.VMEM((PER, cells // 128, rows, 128), jnp.float32),
            pltpu.VMEM(stage, bf16),
            pltpu.VMEM(stage, bf16),
            pltpu.VMEM(stage, bf16),
            pltpu.VMEM(half, bf16),
            pltpu.VMEM(half, bf16),
            pltpu.VMEM(stage, bf16),
            pltpu.VMEM(stage, bf16),
            pltpu.VMEM((STAGES, PER, 2, rows // 2, cells), bf16),
            pltpu.SemaphoreType.DMA((9,)),
            pltpu.SemaphoreType.DMA((2, STAGES)),
            pltpu.SemaphoreType.DMA((2, STAGES)),
            pltpu.SemaphoreType.DMA((2, STAGES)),
            pltpu.SemaphoreType.DMA((2, STAGES)),
            pltpu.SemaphoreType.DMA((STAGES, 2)),
            pltpu.SemaphoreType.DMA((STAGES, 2)),
        ],
        compiler_params=pltpu.CompilerParams(
            collective_id=0, has_side_effects=True, vmem_limit_bytes=44 << 20
        ),
        name="grid_exchange",
    )(
        block_ids[0].T, kernel_ids[0].T, tile_counts,
        visibilities.reshape(blocks, rows, length), kernels,
    )
    nchan = n_chan * ch_dev
    tiles = wedge_mask.shape[0]
    vmem = pl.BlockSpec(memory_space=pltpu.VMEM)
    result = (tiles, 2, cells, nchan)
    return pl.pallas_call(
        delay_kernel,
        out_shape=jax.ShapeDtypeStruct(result, jnp.float32),
        in_specs=[vmem, vmem, vmem],
        out_specs=hbm,
        scratch_shapes=[
            pltpu.VMEM((tiles, 2, cells, nchan), bf16),
            pltpu.VMEM(result, jnp.float32),
            pltpu.SemaphoreType.DMA((4 * tiles * nchan // 2 // cells,)),
        ],
        compiler_params=pltpu.CompilerParams(vmem_limit_bytes=34 << 20),
        cost_estimate=pl.CostEstimate(
            flops=tiles * 4 * cells * nchan * nchan, bytes_accessed=25 << 20, transcendentals=0
        ),
        name="delay_transform",
    )(grids.reshape(2, 2, nchan, cells), table, wedge_mask)


def solution(mesh):
    def run(visibilities, *rest):
        nchan = visibilities.shape[1]
        table = tables(nchan, nchan // mesh.shape["chan"])
        return jax.shard_map(
            functools.partial(
                local, mesh.shape["chan"], mesh.shape["bl"],
                jnp.asarray(table),
            ),
            mesh=mesh,
            in_specs=(
                P("bl", "chan", None, None),
                P(),
                P("bl", None, None),
                P("bl", None, None),
                P("bl", None),
                P(("chan", "bl"), None),
            ),
            out_specs=P(("chan", "bl"), None, None, None),
            check_vma=False,
        )(visibilities, *rest)

    return run
```

```python
import functools
import math

import jax
import jax.numpy as jnp
import ml_dtypes
import numpy as np
from jax import lax
from jax.experimental import pallas as pl
from jax.experimental.pallas import tpu as pltpu
from jax.sharding import PartitionSpec as P

MESH = pl.DeviceIdType.MESH
STAGES = 16
PER = 4


def tables(nchan, ch_dev):
    half = nchan // 2
    delays = np.arange(half, dtype=np.int64)
    result = []
    for odd in range(2):
        chans = np.arange(nchan, dtype=np.int64).reshape(nchan // ch_dev, ch_dev)[:, odd::2]
        phase = chans[:, :, None] * delays % nchan
        angle = phase.astype(np.float32) * np.float32(2.0 * math.pi / nchan)
        cosine, sine = np.cos(angle), np.sin(angle)
        real = np.stack([cosine, sine], axis=1)
        imag = np.stack([-sine, cosine], axis=1)
        both = np.concatenate([real, imag], axis=3).reshape(nchan, nchan)
        result.append(both.astype(ml_dtypes.bfloat16))
    return np.stack(result)


def grid_kernel(
    n_chan, n_bl, bid_hbm, kid_hbm, cnt_hbm, vis_hbm, ker_hbm, grid_out,
    bid, kid, cnt, bid_in, kid_in, cnt_in, bid_out, kid_out, cnt_out,
    vis_hub, vis_leaf, vis_in, ker, sums,
    sum_own, sum_inner, sum_far, sum_outer,
    to_inner, to_far, to_outer, from_inner, from_far, from_outer, own,
    load_sem, vis_s, vis_r, nbr_s, nbr_r, own_s, own_r,
):
    chan = lax.axis_index("chan")
    y = lax.axis_index("bl")
    core = lax.rem(chan, 2)
    col = lax.rem(lax.div(chan, 2), 4)
    row = lax.div(chan, 8)

    role = lax.rem(y + n_bl - core, n_bl)
    hub = lax.rem(lax.div(role + 1, 2) + 1, 2)
    turn = 2 * lax.rem(role, 2)
    outer = lax.rem(y + 1 + turn, n_bl)
    inner = lax.rem(y + 3 + turn, n_bl)
    far = lax.rem(y + 2, n_bl)

    blocks, part_rows = vis_hub.shape[:2]
    kinds = ker_hbm.shape[0]
    hub_at = pl.multiple_of(hub * part_rows, part_rows)
    leaf_at = pl.multiple_of((1 - hub) * part_rows, part_rows)
    cut = blocks // 4

    loads = [
        pltpu.make_async_copy(src, dst, load_sem.at[q])
        for q, (src, dst) in enumerate(
            (
                (bid_hbm, bid), (kid_hbm, kid), (cnt_hbm, cnt),
                (ker_hbm, ker.at[pl.ds(0, kinds)]),
                (vis_hbm.at[:, pl.ds(hub_at, part_rows)], vis_hub),
                (vis_hbm.at[:, pl.ds(leaf_at, part_rows)], vis_leaf),
            )
        )
    ]
    for one in loads:
        one.start()
    ker[kinds] = jnp.zeros(ker.shape[1:], ker.dtype)

    barrier = pltpu.get_barrier_semaphore()

    def greet(o, carry):
        pl.semaphore_signal(
            barrier, inc=1, device_id=(lax.rem(chan + o, n_chan), y), device_id_type=MESH
        )
        return carry

    for other in (outer, inner):
        pl.semaphore_signal(barrier, inc=1, device_id=(chan, other), device_id_type=MESH)
    lax.fori_loop(1, n_chan, greet, 0)
    pl.semaphore_wait(barrier, n_chan + 1)

    def remote(src, dst, send, recv, plane):
        return pltpu.make_async_remote_copy(
            src_ref=src, dst_ref=dst, send_sem=send, recv_sem=recv,
            device_id=(chan, plane), device_id_type=MESH,
        )

    vis_copies = [
        remote(src, dst, vis_s.at[q], vis_r.at[q], outer)
        for q, (src, dst) in enumerate(
            [(bid_hbm, bid_in), (kid_hbm, kid_in), (cnt_hbm, cnt_in)]
            + [
                (
                    vis_hbm.at[pl.ds(q * cut, cut), pl.ds(leaf_at, part_rows)],
                    vis_in.at[pl.ds(q * cut, cut)],
                )
                for q in range(4)
            ]
        )
    ]
    for copy in vis_copies:
        copy.start()
    for one in loads:
        one.wait()

    def owner(s, e):
        m = STAGES - 1 - s
        dz = lax.rem(m, 4)
        dx = lax.rem(lax.div(m, 4) + m, 4)
        return (lax.rem(row + dz, 4) * 4 + lax.rem(col + dx, 4)) * 2 + lax.rem(core + e, 2)

    def tile_of(s, j, plane):
        return (owner(s, j // 2) * n_bl + plane) * 2 + j % 2

    def partial(tile, ids, sources):
        block_of, kind_of, count_of = ids
        count = count_of[0, tile]
        left_side, right_side = [], []
        for k in range(8):
            b = block_of[k, tile]
            q = jnp.where(k < count, kind_of[k, tile], kinds)
            chosen = [one[b] for one in sources]
            left_side.append(chosen[0] if len(chosen) == 1 else jnp.concatenate(chosen, axis=0))
            right_side.append(ker[q])
        return jnp.dot(
            jnp.concatenate(left_side, axis=1),
            jnp.concatenate(right_side, axis=0),
            preferred_element_type=jnp.float32,
        )

    mine = (bid, kid, cnt)
    others = (bid_out, kid_out, cnt_out)

    def first(s, carry):
        for j in range(PER):
            sum_far[s, j] = partial(tile_of(s, j, far), mine, [vis_hub])
            sum_inner[s, j] = partial(tile_of(s, j, inner), mine, [vis_hub])
            sum_outer[s, j] = partial(tile_of(s, j, outer), mine, [vis_hub])
            sum_own[s, j] = partial(tile_of(s, j, y), mine, [vis_hub, vis_leaf])
        return carry

    lax.fori_loop(0, STAGES, first, 0)

    for copy in vis_copies:
        copy.wait_recv()
    arrived = [
        pltpu.make_async_copy(src, dst, load_sem.at[q])
        for q, (src, dst) in enumerate(((bid_in, bid_out), (kid_in, kid_out), (cnt_in, cnt_out)))
    ]
    for one in arrived:
        one.start()
    for one in arrived:
        one.wait()

    def far_copy(s):
        return remote(to_far.at[s], from_far.at[s], nbr_s.at[0, s], nbr_r.at[0, s], inner)

    def inner_copy(s):
        return remote(to_inner.at[s], from_inner.at[s], nbr_s.at[1, s], nbr_r.at[1, s], inner)

    def outer_copy(s):
        return remote(to_outer.at[s], from_outer.at[s], nbr_s.at[2, s], nbr_r.at[2, s], outer)

    def own_copy(s, e):
        return pltpu.make_async_remote_copy(
            src_ref=own.at[s, pl.ds(2 * e, 2)],
            dst_ref=grid_out.at[:, :, chan],
            send_sem=own_s.at[s, e], recv_sem=own_r.at[s, e],
            device_id=(owner(s, e), y), device_id_type=MESH,
        )

    def self_copy():
        return pltpu.make_async_copy(
            own.at[STAGES - 1, pl.ds(0, 2)], grid_out.at[:, :, chan], own_r.at[STAGES - 1, 0]
        )

    def step(it, carry):
        @pl.when(it < STAGES)
        def _():
            s = it
            for j in range(PER):
                to_far[s, j] = (
                    sum_far[s, j] + partial(tile_of(s, j, far), others, [vis_in])
                ).astype(jnp.bfloat16)
            far_copy(s).start()
            for j in range(PER):
                to_inner[s, j] = (
                    sum_inner[s, j] + partial(tile_of(s, j, inner), others, [vis_in])
                ).astype(jnp.bfloat16)
            inner_copy(s).start()

        @pl.when((it >= 1) & (it < STAGES + 1))
        def _():
            s = it - 1
            far_copy(s).wait_recv()
            for j in range(PER):
                to_outer[s, j] = (
                    sum_outer[s, j] + from_far[s, j].astype(jnp.float32)
                ).astype(jnp.bfloat16)
            outer_copy(s).start()

        @pl.when(it >= 2)
        def _():
            s = it - 2
            inner_copy(s).wait_recv()
            outer_copy(s).wait_recv()
            for j in range(PER):
                hub_rows = (
                    sum_own[s, j, :part_rows]
                    + partial(tile_of(s, j, y), others, [vis_in])
                    + from_inner[s, j].astype(jnp.float32)
                )
                leaf_rows = sum_own[s, j, part_rows:] + from_outer[s, j].astype(jnp.float32)
                for lane in range(sums.shape[1]):
                    at = slice(lane * 128, lane * 128 + 128)
                    sums[j, lane, pl.ds(hub_at, part_rows)] = hub_rows[:, at]
                    sums[j, lane, pl.ds(leaf_at, part_rows)] = leaf_rows[:, at]
                for odd in range(2):
                    sorted_rows = [
                        jnp.concatenate(
                            [
                                sums[j, lane, pl.ds(2 * odd + p, part_rows // 2, stride=4)]
                                for p in range(2)
                            ],
                            axis=0,
                        )
                        for lane in range(sums.shape[1])
                    ]
                    own[s, j, odd] = jnp.concatenate(sorted_rows, axis=1).astype(jnp.bfloat16)

            @pl.when(s < STAGES - 1)
            def _():
                own_copy(s, 0).start()

            own_copy(s, 1).start()

            @pl.when(s == STAGES - 1)
            def _():
                self_copy().start()

        return carry

    lax.fori_loop(0, STAGES + 2, step, 0)

    for copy in vis_copies:
        copy.wait_send()

    def drain(s, carry):
        for copy in (far_copy(s), inner_copy(s), outer_copy(s)):
            copy.wait_send()

        @pl.when(s < STAGES - 1)
        def _():
            own_copy(s, 0).wait()

        own_copy(s, 1).wait()
        return carry

    lax.fori_loop(0, STAGES, drain, 0)
    self_copy().wait()


def delay_kernel(grids, table, keep, out_hbm, left, out, sem):
    tiles, parities, nchan, cells = grids.shape
    half = nchan // 2
    width = cells
    scale = 1.0 / math.sqrt(nchan)
    copies = []
    for t in range(tiles):
        for odd in range(parities):
            left[t, odd] = grids[t, odd].T
        for part in range(2):
            for q in range(half // width):
                at = part * half + q * width
                even_sum, odd_sum = (
                    jnp.dot(
                        left[t, odd], table[odd, :, at : at + width],
                        preferred_element_type=jnp.float32,
                    )
                    for odd in range(2)
                )
                for side, value in enumerate((even_sum + odd_sum, even_sum - odd_sum)):
                    lane = side * half + q * width
                    bins = keep[t : t + 1, lane : lane + width].astype(jnp.float32) * scale
                    out[t, part, :, lane : lane + width] = value * bins
                    copy = pltpu.make_async_copy(
                        out.at[t, part, :, pl.ds(lane, width)],
                        out_hbm.at[t, part, :, pl.ds(lane, width)],
                        sem.at[len(copies)],
                    )
                    copy.start()
                    copies.append(copy)
    for copy in copies:
        copy.wait()


def local(n_chan, n_bl, table, visibilities, kernels, block_ids, kernel_ids, tile_counts, wedge_mask):
    blocks, ch_dev = visibilities.shape[:2]
    length, cells = kernels.shape[1:]
    rows = ch_dev * 2
    bf16 = jnp.bfloat16
    part_rows = rows // 2
    stage = (STAGES, PER, part_rows, cells)
    f32 = jnp.float32
    hbm = pl.BlockSpec(memory_space=pltpu.HBM)
    ids = (block_ids.shape[2], block_ids.shape[1])
    operands = (
        block_ids[0].T, kernel_ids[0].T, tile_counts,
        visibilities.reshape(blocks, rows, length), kernels,
    )
    grids = pl.pallas_call(
        functools.partial(grid_kernel, n_chan, n_bl),
        out_shape=jax.ShapeDtypeStruct((2, 2, n_chan, part_rows, cells), bf16),
        in_specs=[hbm] * len(operands),
        out_specs=pl.BlockSpec(memory_space=pl.ANY),
        scratch_shapes=[
            pltpu.SMEM(ids, jnp.int32),
            pltpu.SMEM(ids, jnp.int32),
            pltpu.SMEM(tile_counts.shape, jnp.int32),
            pltpu.VMEM(ids, jnp.int32),
            pltpu.VMEM(ids, jnp.int32),
            pltpu.VMEM(tile_counts.shape, jnp.int32),
            pltpu.SMEM(ids, jnp.int32),
            pltpu.SMEM(ids, jnp.int32),
            pltpu.SMEM(tile_counts.shape, jnp.int32),
            pltpu.VMEM((blocks, part_rows, length), bf16),
            pltpu.VMEM((blocks, part_rows, length), bf16),
            pltpu.VMEM((blocks, part_rows, length), bf16),
            pltpu.VMEM((kernels.shape[0] + 1, length, cells), bf16),
            pltpu.VMEM((PER, cells // 128, rows, 128), f32),
            pltpu.VMEM((STAGES, PER, rows, cells), f32),
            pltpu.VMEM(stage, f32),
            pltpu.VMEM(stage, f32),
            pltpu.VMEM(stage, f32),
            pltpu.VMEM(stage, bf16),
            pltpu.VMEM(stage, bf16),
            pltpu.VMEM(stage, bf16),
            pltpu.VMEM(stage, bf16),
            pltpu.VMEM(stage, bf16),
            pltpu.VMEM(stage, bf16),
            pltpu.VMEM((STAGES, PER, 2, part_rows, cells), bf16),
            pltpu.SemaphoreType.DMA((6,)),
            pltpu.SemaphoreType.DMA((7,)),
            pltpu.SemaphoreType.DMA((7,)),
            pltpu.SemaphoreType.DMA((3, STAGES)),
            pltpu.SemaphoreType.DMA((3, STAGES)),
            pltpu.SemaphoreType.DMA((STAGES, 2)),
            pltpu.SemaphoreType.DMA((STAGES, 2)),
        ],
        compiler_params=pltpu.CompilerParams(
            collective_id=0, has_side_effects=True, vmem_limit_bytes=48 << 20
        ),
        name="grid_exchange",
    )(*(pltpu.with_memory_space_constraint(one, pltpu.HBM) for one in operands))
    nchan = n_chan * ch_dev
    tiles = wedge_mask.shape[0]
    vmem = pl.BlockSpec(memory_space=pltpu.VMEM)
    result = (tiles, 2, cells, nchan)
    return pl.pallas_call(
        delay_kernel,
        out_shape=jax.ShapeDtypeStruct(result, jnp.float32),
        in_specs=[vmem, vmem, vmem],
        out_specs=hbm,
        scratch_shapes=[
            pltpu.VMEM((tiles, 2, cells, nchan), bf16),
            pltpu.VMEM(result, jnp.float32),
            pltpu.SemaphoreType.DMA((4 * tiles * nchan // 2 // cells,)),
        ],
        compiler_params=pltpu.CompilerParams(vmem_limit_bytes=34 << 20),
        cost_estimate=pl.CostEstimate(
            flops=tiles * 4 * cells * nchan * nchan, bytes_accessed=25 << 20, transcendentals=0
        ),
        name="delay_transform",
    )(grids.reshape(2, 2, nchan, cells), table, wedge_mask)


def solution(mesh):
    def run(visibilities, *rest):
        nchan = visibilities.shape[1]
        table = tables(nchan, nchan // mesh.shape["chan"])
        return jax.shard_map(
            functools.partial(
                local, mesh.shape["chan"], mesh.shape["bl"],
                jnp.asarray(table),
            ),
            mesh=mesh,
            in_specs=(
                P("bl", "chan", None, None),
                P(),
                P("bl", None, None),
                P("bl", None, None),
                P("bl", None),
                P(("chan", "bl"), None),
            ),
            out_specs=P(("chan", "bl"), None, None, None),
            check_vma=False,
        )(visibilities, *rest)

    return run
```

```python
import functools
import math

import jax
import jax.numpy as jnp
import ml_dtypes
import numpy as np
from jax import lax
from jax.experimental import pallas as pl
from jax.experimental.pallas import tpu as pltpu
from jax.sharding import PartitionSpec as P

MESH = pl.DeviceIdType.MESH
STAGES = 32
OFFSETS = (
    (0, 0), (0, 1), (3, 0), (0, 3), (1, 0), (1, 1), (3, 3), (0, 2),
    (1, 3), (3, 1), (2, 0), (1, 2), (2, 3), (3, 2), (2, 1), (2, 2),
)
PER = 2
LAG = 3
OWN_LAG = 6
SLICE_AT = STAGES // 2 + OWN_LAG + 1


def tables(nchan, ch_dev):
    half = nchan // 2
    delays = np.arange(half, dtype=np.int64)
    result = []
    for odd in range(2):
        chans = np.arange(nchan, dtype=np.int64).reshape(nchan // ch_dev, ch_dev)[:, odd::2]
        phase = chans[:, :, None] * delays % nchan
        angle = phase.astype(np.float32) * np.float32(2.0 * math.pi / nchan)
        cosine, sine = np.cos(angle), np.sin(angle)
        real = np.stack([cosine, sine], axis=1)
        imag = np.stack([-sine, cosine], axis=1)
        both = np.concatenate([real, imag], axis=3).reshape(nchan, nchan)
        result.append(both.astype(ml_dtypes.bfloat16))
    return np.stack(result)


def grid_kernel(
    n_chan, n_bl, bid_hbm, kid_hbm, cnt_hbm, vis_hbm, ker_hbm, table_hbm, keep_hbm, grid_out, out,
    bid, kid, cnt, bid_in, kid_in, cnt_in, bid_out, kid_out, cnt_out,
    vis_hub, vis_leaf, vis_in, ker, sums,
    sum_own, sum_inner, sum_far, sum_outer,
    to_inner, to_far, to_outer, from_inner, from_far, from_outer, own,
    grid_first, left, table, keep,
    load_sem, vis_s, vis_r, nbr_s, nbr_r, own_s, own_r,
):
    chan = lax.axis_index("chan")
    y = lax.axis_index("bl")
    core = lax.rem(chan, 2)
    col = lax.rem(lax.div(chan, 2), 4)
    row = lax.div(chan, 8)

    role = lax.rem(y + n_bl - core, n_bl)
    hub = lax.rem(lax.div(role + 1, 2) + 1, 2)
    turn = 2 * lax.rem(role, 2)
    outer = lax.rem(y + 1 + turn, n_bl)
    inner = lax.rem(y + 3 + turn, n_bl)
    far = lax.rem(y + 2, n_bl)

    blocks, part_rows = vis_hub.shape[:2]
    kinds = ker_hbm.shape[0]
    hub_at = pl.multiple_of(hub * part_rows, part_rows)
    leaf_at = pl.multiple_of((1 - hub) * part_rows, part_rows)
    cut = blocks // 4

    loads = [
        pltpu.make_async_copy(src, dst, load_sem.at[q])
        for q, (src, dst) in enumerate(
            (
                (bid_hbm, bid), (kid_hbm, kid), (cnt_hbm, cnt),
                (ker_hbm, ker.at[pl.ds(0, kinds)]),
                (vis_hbm.at[:, pl.ds(hub_at, part_rows)], vis_hub),
                (vis_hbm.at[:, pl.ds(leaf_at, part_rows)], vis_leaf),
            )
        )
    ]
    for one in loads:
        one.start()
    ker[kinds] = jnp.zeros(ker.shape[1:], ker.dtype)

    barrier = pltpu.get_barrier_semaphore()

    def greet(o, carry):
        pl.semaphore_signal(
            barrier, inc=1, device_id=(lax.rem(chan + o, n_chan), y), device_id_type=MESH
        )
        return carry

    for other in (outer, inner):
        pl.semaphore_signal(barrier, inc=1, device_id=(chan, other), device_id_type=MESH)
    lax.fori_loop(1, n_chan, greet, 0)
    pl.semaphore_wait(barrier, n_chan + 1)

    def remote(src, dst, send, recv, plane):
        return pltpu.make_async_remote_copy(
            src_ref=src, dst_ref=dst, send_sem=send, recv_sem=recv,
            device_id=(chan, plane), device_id_type=MESH,
        )

    vis_copies = [
        remote(src, dst, vis_s.at[q], vis_r.at[q], outer)
        for q, (src, dst) in enumerate(
            [(bid_hbm, bid_in), (kid_hbm, kid_in), (cnt_hbm, cnt_in)]
            + [
                (
                    vis_hbm.at[pl.ds(q * cut, cut), pl.ds(leaf_at, part_rows)],
                    vis_in.at[pl.ds(q * cut, cut)],
                )
                for q in range(4)
            ]
        )
    ]
    for copy in vis_copies:
        copy.start()
    for one in loads:
        one.wait()
    late = [
        pltpu.make_async_copy(src, dst, load_sem.at[6 + q])
        for q, (src, dst) in enumerate(((keep_hbm, keep), (table_hbm, table)))
    ]
    for one in late:
        one.start()
    for copy in vis_copies[:3]:
        copy.wait_recv()
    arrived = [
        pltpu.make_async_copy(src, dst, load_sem.at[q])
        for q, (src, dst) in enumerate(((bid_in, bid_out), (kid_in, kid_out), (cnt_in, cnt_out)))
    ]
    for one in arrived:
        one.start()
    for one in arrived:
        one.wait()

    half = STAGES // 2

    def owner(s, e):
        m = half - 1 - lax.rem(s, half)
        dz, dx = 0, 0
        for at, (first_of, second_of) in enumerate(OFFSETS):
            dz = jnp.where(m == at, first_of, dz)
            dx = jnp.where(m == at, second_of, dx)
        return (lax.rem(row + dz, 4) * 4 + lax.rem(col + dx, 4)) * 2 + lax.rem(core + e, 2)

    def tile_of(s, j, plane):
        return (owner(s, j) * n_bl + plane) * 2 + lax.div(s, half)

    def partial(tile, ids, sources):
        block_of, kind_of, count_of = ids
        count = count_of[0, tile]
        left_side, right_side = [], []
        for k in range(8):
            b = block_of[k, tile]
            q = jnp.where(k < count, kind_of[k, tile], kinds)
            chosen = [one[b] for one in sources]
            left_side.append(chosen[0] if len(chosen) == 1 else jnp.concatenate(chosen, axis=0))
            right_side.append(ker[q])
        return jnp.dot(
            jnp.concatenate(left_side, axis=1),
            jnp.concatenate(right_side, axis=0),
            preferred_element_type=jnp.float32,
        )

    mine = (bid, kid, cnt)
    others = (bid_out, kid_out, cnt_out)

    def first(s, carry):
        for j in range(PER):
            for plane, kept, sources in (
                (far, sum_far, [vis_hub]),
                (inner, sum_inner, [vis_hub]),
                (outer, sum_outer, [vis_hub]),
                (y, sum_own, [vis_hub, vis_leaf]),
            ):
                kept[s, j] = partial(tile_of(s, j, plane), mine, sources).astype(kept.dtype)
        return carry

    lax.fori_loop(0, STAGES, first, 0)

    for one in late:
        one.wait()
    for copy in vis_copies[3:]:
        copy.wait_recv()

    def far_copy(s):
        return remote(to_far.at[s], from_far.at[s], nbr_s.at[0, s], nbr_r.at[0, s], inner)

    def inner_copy(s):
        return remote(to_inner.at[s], from_inner.at[s], nbr_s.at[1, s], nbr_r.at[1, s], inner)

    def outer_copy(s):
        return remote(to_outer.at[s], from_outer.at[s], nbr_s.at[2, s], nbr_r.at[2, s], outer)

    def own_copy(s, e, target):
        return pltpu.make_async_remote_copy(
            src_ref=own.at[s, e], dst_ref=target.at[:, chan],
            send_sem=own_s.at[s, e], recv_sem=own_r.at[s, e],
            device_id=(owner(s, e), y), device_id_type=MESH,
        )

    def self_copy(s, target):
        return pltpu.make_async_copy(own.at[s, 0], target.at[:, chan], own_r.at[s, 0])

    def send_own(s, target, last):
        @pl.when(s < last)
        def _():
            own_copy(s, 0, target).start()

        own_copy(s, 1, target).start()

        @pl.when(s == last)
        def _():
            self_copy(last, target).start()

    nchan, width = left.shape[2], left.shape[1]
    slices = nchan // 2 // width

    def lanes_of(q):
        return [pl.multiple_of(side * (nchan // 2) + q * width, width) for side in range(2)]

    def step(it, carry):
        @pl.when(it < STAGES)
        def _():
            s = it
            for j in range(PER):
                to_far[s, j] = (
                    sum_far[s, j].astype(jnp.float32) + partial(tile_of(s, j, far), others, [vis_in])
                ).astype(jnp.bfloat16)
            far_copy(s).start()

        @pl.when((it >= LAG) & (it < STAGES + LAG))
        def _():
            s = it - LAG
            for j in range(PER):
                to_inner[s, j] = (
                    sum_inner[s, j].astype(jnp.float32) + partial(tile_of(s, j, inner), others, [vis_in])
                ).astype(jnp.bfloat16)
            inner_copy(s).start()
            far_copy(s).wait_recv()
            for j in range(PER):
                to_outer[s, j] = (
                    sum_outer[s, j].astype(jnp.float32) + from_far[s, j].astype(jnp.float32)
                ).astype(jnp.bfloat16)
            outer_copy(s).start()

        @pl.when(it >= OWN_LAG)
        def _():
            s = it - OWN_LAG
            inner_copy(s).wait_recv()
            outer_copy(s).wait_recv()
            for j in range(PER):
                hub_rows = (
                    sum_own[s, j, :part_rows].astype(jnp.float32)
                    + partial(tile_of(s, j, y), others, [vis_in])
                    + from_inner[s, j].astype(jnp.float32)
                )
                leaf_rows = sum_own[s, j, part_rows:].astype(jnp.float32) + from_outer[s, j].astype(jnp.float32)
                for lane in range(sums.shape[1]):
                    at = slice(lane * 128, lane * 128 + 128)
                    sums[j, lane, pl.ds(hub_at, part_rows)] = hub_rows[:, at]
                    sums[j, lane, pl.ds(leaf_at, part_rows)] = leaf_rows[:, at]
                for odd in range(2):
                    sorted_rows = [
                        jnp.concatenate(
                            [
                                sums[j, lane, pl.ds(2 * odd + p, part_rows // 2, stride=4)]
                                for p in range(2)
                            ],
                            axis=0,
                        )
                        for lane in range(sums.shape[1])
                    ]
                    own[s, j, odd] = jnp.concatenate(sorted_rows, axis=1).astype(jnp.bfloat16)

            @pl.when(s < half)
            def _():
                send_own(s, grid_first, half - 1)

            @pl.when(s >= half)
            def _():
                send_own(s, grid_out, STAGES - 1)

        @pl.when(it == SLICE_AT)
        def _():
            def received(s, c):
                @pl.when(s < half - 1)
                def _():
                    own_copy(s, 0, grid_first).wait_recv()

                own_copy(s, 1, grid_first).wait_recv()
                return c

            lax.fori_loop(0, half, received, 0)
            self_copy(half - 1, grid_first).wait()

        @pl.when((it >= SLICE_AT) & (it < SLICE_AT + 2))
        def _():
            odd = it - SLICE_AT
            left[odd] = grid_first[odd].reshape(nchan, width).T

        @pl.when((it >= SLICE_AT + 2) & (it < SLICE_AT + 2 + 2 * slices))
        def _():
            c = it - SLICE_AT - 2
            part, q = lax.div(c, slices), lax.rem(c, slices)
            at = pl.multiple_of(part * (nchan // 2) + q * width, width)
            values = delay_slice(
                [left[odd] for odd in range(2)],
                [table[odd, :, pl.ds(at, width)] for odd in range(2)],
            )
            for lane, value in zip(lanes_of(q), values):
                bins = keep[0:1, pl.ds(lane, width)].astype(jnp.float32) * (1.0 / math.sqrt(nchan))
                out[part, :, pl.ds(lane, width)] = value * bins

        return carry

    lax.fori_loop(0, STAGES + OWN_LAG, step, 0)

    for copy in vis_copies:
        copy.wait_send()

    def drain(s, carry):
        for copy in (far_copy(s), inner_copy(s), outer_copy(s)):
            copy.wait_send()

        @pl.when(s < half)
        def _():
            @pl.when(s < half - 1)
            def _():
                own_copy(s, 0, grid_first).wait_send()

            own_copy(s, 1, grid_first).wait_send()

        @pl.when(s >= half)
        def _():
            @pl.when(s < STAGES - 1)
            def _():
                own_copy(s, 0, grid_out).wait()

            own_copy(s, 1, grid_out).wait()

        return carry

    lax.fori_loop(0, STAGES, drain, 0)
    self_copy(STAGES - 1, grid_out).wait()


def delay_slice(left, right):
    even_sum, odd_sum = (
        jnp.dot(one, two, preferred_element_type=jnp.float32) for one, two in zip(left, right)
    )
    return even_sum + odd_sum, even_sum - odd_sum


def delay_kernel(grids, table, keep, first_tile, out_hbm, left, out, sem, first_sem):
    parities, nchan, cells = grids.shape
    half = nchan // 2
    width = cells
    scale = 1.0 / math.sqrt(nchan)
    copies = []
    for part in range(2):
        copy = pltpu.make_async_copy(first_tile.at[part], out_hbm.at[0, part], first_sem.at[part])
        copy.start()
        copies.append(copy)
    for odd in range(parities):
        left[odd] = grids[odd].T
    for part in range(2):
        for q in range(half // width):
            at = part * half + q * width
            values = delay_slice(
                [left[odd] for odd in range(2)],
                [table[odd, :, at : at + width] for odd in range(2)],
            )
            for side, value in enumerate(values):
                lane = side * half + q * width
                bins = keep[1:2, lane : lane + width].astype(jnp.float32) * scale
                out[part, :, lane : lane + width] = value * bins
                copy = pltpu.make_async_copy(
                    out.at[part, :, pl.ds(lane, width)],
                    out_hbm.at[1, part, :, pl.ds(lane, width)],
                    sem.at[2 * (part * (half // width) + q) + side],
                )
                copy.start()
                copies.append(copy)
    for copy in copies:
        copy.wait()


def local(n_chan, n_bl, table, visibilities, kernels, block_ids, kernel_ids, tile_counts, wedge_mask):
    blocks, ch_dev = visibilities.shape[:2]
    length, cells = kernels.shape[1:]
    rows = ch_dev * 2
    bf16 = jnp.bfloat16
    part_rows = rows // 2
    stage = (STAGES, PER, part_rows, cells)
    f32 = jnp.float32
    hbm = pl.BlockSpec(memory_space=pltpu.HBM)
    ids = (block_ids.shape[2], block_ids.shape[1])
    operands = (
        block_ids[0].T, kernel_ids[0].T, tile_counts,
        visibilities.reshape(blocks, rows, length), kernels, table, wedge_mask,
    )
    nchan = n_chan * ch_dev
    tiles = wedge_mask.shape[0]
    result = (tiles, 2, cells, nchan)
    grids, first_tile = pl.pallas_call(
        functools.partial(grid_kernel, n_chan, n_bl),
        out_shape=(
            jax.ShapeDtypeStruct((2, n_chan, part_rows, cells), bf16),
            jax.ShapeDtypeStruct(result[1:], f32),
        ),
        in_specs=[hbm] * len(operands),
        out_specs=(pl.BlockSpec(memory_space=pl.ANY), pl.BlockSpec(memory_space=pltpu.VMEM)),
        scratch_shapes=[
            pltpu.SMEM(ids, jnp.int32),
            pltpu.SMEM(ids, jnp.int32),
            pltpu.SMEM(tile_counts.shape, jnp.int32),
            pltpu.VMEM(ids, jnp.int32),
            pltpu.VMEM(ids, jnp.int32),
            pltpu.VMEM(tile_counts.shape, jnp.int32),
            pltpu.SMEM(ids, jnp.int32),
            pltpu.SMEM(ids, jnp.int32),
            pltpu.SMEM(tile_counts.shape, jnp.int32),
            pltpu.VMEM((blocks, part_rows, length), bf16),
            pltpu.VMEM((blocks, part_rows, length), bf16),
            pltpu.VMEM((blocks, part_rows, length), bf16),
            pltpu.VMEM((kernels.shape[0] + 1, length, cells), bf16),
            pltpu.VMEM((PER, cells // 128, rows, 128), f32),
            pltpu.VMEM((STAGES, PER, rows, cells), bf16),
            pltpu.VMEM(stage, bf16),
            pltpu.VMEM(stage, bf16),
            pltpu.VMEM(stage, bf16),
            pltpu.VMEM(stage, bf16),
            pltpu.VMEM(stage, bf16),
            pltpu.VMEM(stage, bf16),
            pltpu.VMEM(stage, bf16),
            pltpu.VMEM(stage, bf16),
            pltpu.VMEM(stage, bf16),
            pltpu.VMEM((STAGES, PER, 2, part_rows, cells), bf16),
            pltpu.VMEM((2, n_chan, part_rows, cells), bf16),
            pltpu.VMEM((2, cells, nchan), bf16),
            pltpu.VMEM(table.shape, bf16),
            pltpu.VMEM(wedge_mask.shape, jnp.int32),
            pltpu.SemaphoreType.DMA((8,)),
            pltpu.SemaphoreType.DMA((7,)),
            pltpu.SemaphoreType.DMA((7,)),
            pltpu.SemaphoreType.DMA((3, STAGES)),
            pltpu.SemaphoreType.DMA((3, STAGES)),
            pltpu.SemaphoreType.DMA((STAGES, 2)),
            pltpu.SemaphoreType.DMA((STAGES, 2)),
        ],
        compiler_params=pltpu.CompilerParams(
            collective_id=0, has_side_effects=True, vmem_limit_bytes=47 << 20
        ),
        name="grid_exchange",
    )(*(pltpu.with_memory_space_constraint(one, pltpu.HBM) for one in operands))
    vmem = pl.BlockSpec(memory_space=pltpu.VMEM)
    return pl.pallas_call(
        delay_kernel,
        out_shape=jax.ShapeDtypeStruct(result, f32),
        in_specs=[vmem, vmem, vmem, vmem],
        out_specs=hbm,
        scratch_shapes=[
            pltpu.VMEM((2, cells, nchan), bf16),
            pltpu.VMEM(result[1:], f32),
            pltpu.SemaphoreType.DMA((2 * nchan // cells,)),
            pltpu.SemaphoreType.DMA((2,)),
        ],
        compiler_params=pltpu.CompilerParams(vmem_limit_bytes=26 << 20),
        cost_estimate=pl.CostEstimate(
            flops=4 * cells * nchan * nchan, bytes_accessed=16 << 20, transcendentals=0
        ),
        name="delay_transform",
    )(
        grids.reshape(2, nchan, cells), table, wedge_mask,
        first_tile,
    )


def solution(mesh):
    def run(visibilities, *rest):
        nchan = visibilities.shape[1]
        table = tables(nchan, nchan // mesh.shape["chan"])
        return jax.shard_map(
            functools.partial(
                local, mesh.shape["chan"], mesh.shape["bl"],
                jnp.asarray(table),
            ),
            mesh=mesh,
            in_specs=(
                P("bl", "chan", None, None),
                P(),
                P("bl", None, None),
                P("bl", None, None),
                P("bl", None),
                P(("chan", "bl"), None),
            ),
            out_specs=P(("chan", "bl"), None, None, None),
            check_vma=False,
        )(visibilities, *rest)

    return run
```

```python
import functools
import math

import jax
import jax.numpy as jnp
import ml_dtypes
import numpy as np
from jax import lax
from jax.experimental import pallas as pl
from jax.experimental.pallas import tpu as pltpu
from jax.sharding import PartitionSpec as P

MESH = pl.DeviceIdType.MESH
STAGES = 32
OFFSETS = (
    (0, 0), (0, 1), (3, 0), (0, 3), (1, 0), (1, 1), (3, 3), (0, 2),
    (1, 3), (3, 1), (2, 0), (1, 2), (2, 3), (3, 2), (2, 1), (2, 2),
)
PER = 2
LAG = 3
OWN_LAG = 7
SLICE_AT = STAGES // 2 + OWN_LAG + 2


def tables(nchan, ch_dev):
    half = nchan // 2
    delays = np.arange(half, dtype=np.int64)
    result = []
    for odd in range(2):
        chans = np.arange(nchan, dtype=np.int64).reshape(nchan // ch_dev, ch_dev)[:, odd::2]
        phase = chans[:, :, None] * delays % nchan
        angle = phase.astype(np.float32) * np.float32(2.0 * math.pi / nchan)
        cosine, sine = np.cos(angle), np.sin(angle)
        real = np.stack([cosine, sine], axis=1)
        imag = np.stack([-sine, cosine], axis=1)
        both = np.concatenate([real, imag], axis=3).reshape(nchan, nchan)
        result.append(both.astype(ml_dtypes.bfloat16))
    return np.stack(result)


def grid_kernel(
    n_chan, n_bl, bid_hbm, kid_hbm, cnt_hbm, vis_hbm, ker_hbm, table_hbm, keep_hbm, grid_out, out,
    bid, kid, cnt, bid_in, kid_in, cnt_in, bid_out, kid_out, cnt_out,
    vis_hub, vis_leaf, vis_in, ker, sums,
    sum_own, sum_inner, sum_far, sum_outer,
    to_inner, to_far, to_outer, from_inner, from_far, from_outer, own,
    grid_first, left, table, keep,
    load_sem, vis_s, vis_r, nbr_s, nbr_r, own_s, own_r,
):
    chan = lax.axis_index("chan")
    y = lax.axis_index("bl")
    core = lax.rem(chan, 2)
    col = lax.rem(lax.div(chan, 2), 4)
    row = lax.div(chan, 8)

    role = lax.rem(y + n_bl - core, n_bl)
    hub = lax.rem(lax.div(role + 1, 2) + 1, 2)
    turn = 2 * lax.rem(role, 2)
    outer = lax.rem(y + 1 + turn, n_bl)
    inner = lax.rem(y + 3 + turn, n_bl)
    far = lax.rem(y + 2, n_bl)

    blocks, part_rows = vis_hub.shape[:2]
    kinds = ker_hbm.shape[0]
    hub_at = pl.multiple_of(hub * part_rows, part_rows)
    leaf_at = pl.multiple_of((1 - hub) * part_rows, part_rows)
    cut = blocks // 4

    barrier = pltpu.get_barrier_semaphore()

    def greet(o, carry):
        pl.semaphore_signal(
            barrier, inc=1, device_id=(lax.rem(chan + o, n_chan), y), device_id_type=MESH
        )
        return carry

    for other in (outer, inner):
        pl.semaphore_signal(barrier, inc=1, device_id=(chan, other), device_id_type=MESH)
    lax.fori_loop(1, n_chan, greet, 0, unroll=True)
    loads = [
        pltpu.make_async_copy(src, dst, load_sem.at[q])
        for q, (src, dst) in enumerate(
            (
                (bid_hbm, bid), (kid_hbm, kid), (cnt_hbm, cnt),
                (ker_hbm, ker.at[pl.ds(0, kinds)]),
                (vis_hbm.at[:, pl.ds(hub_at, part_rows)], vis_hub),
                (vis_hbm.at[:, pl.ds(leaf_at, part_rows)], vis_leaf),
            )
        )
    ]
    for one in loads:
        one.start()
    ker[kinds] = jnp.zeros(ker.shape[1:], ker.dtype)

    pl.semaphore_wait(barrier, n_chan + 1)

    def remote(src, dst, send, recv, plane):
        return pltpu.make_async_remote_copy(
            src_ref=src, dst_ref=dst, send_sem=send, recv_sem=recv,
            device_id=(chan, plane), device_id_type=MESH,
        )

    vis_copies = [
        remote(src, dst, vis_s.at[q], vis_r.at[q], outer)
        for q, (src, dst) in enumerate(
            [(bid_hbm, bid_in), (kid_hbm, kid_in), (cnt_hbm, cnt_in)]
            + [
                (
                    vis_hbm.at[pl.ds(q * cut, cut), pl.ds(leaf_at, part_rows)],
                    vis_in.at[pl.ds(q * cut, cut)],
                )
                for q in range(4)
            ]
        )
    ]
    for copy in vis_copies:
        copy.start()
    for one in loads:
        one.wait()
    late = [
        pltpu.make_async_copy(src, dst, load_sem.at[6 + q])
        for q, (src, dst) in enumerate(((keep_hbm, keep), (table_hbm, table)))
    ]
    for one in late:
        one.start()
    for copy in vis_copies[:3]:
        copy.wait_recv()
    arrived = [
        pltpu.make_async_copy(src, dst, load_sem.at[q])
        for q, (src, dst) in enumerate(((bid_in, bid_out), (kid_in, kid_out), (cnt_in, cnt_out)))
    ]
    for one in arrived:
        one.start()
    for one in arrived:
        one.wait()

    half = STAGES // 2

    def owner(s, e):
        m = half - 1 - lax.rem(s, half)
        dz, dx = 0, 0
        for at, (first_of, second_of) in enumerate(OFFSETS):
            dz = jnp.where(m == at, first_of, dz)
            dx = jnp.where(m == at, second_of, dx)
        return (lax.rem(row + dz, 4) * 4 + lax.rem(col + dx, 4)) * 2 + lax.rem(core + e, 2)

    def tile_of(s, j, plane):
        return (owner(s, j) * n_bl + plane) * 2 + lax.div(s, half)

    def partial(tile, ids, sources):
        block_of, kind_of, count_of = ids
        count = count_of[0, tile]
        left_side, right_side = [], []
        for k in range(8):
            b = block_of[k, tile]
            q = jnp.where(k < count, kind_of[k, tile], kinds)
            chosen = [one[b] for one in sources]
            left_side.append(chosen[0] if len(chosen) == 1 else jnp.concatenate(chosen, axis=0))
            right_side.append(ker[q])
        return jnp.dot(
            jnp.concatenate(left_side, axis=1),
            jnp.concatenate(right_side, axis=0),
            preferred_element_type=jnp.float32,
        )

    mine = (bid, kid, cnt)
    others = (bid_out, kid_out, cnt_out)

    def first(s, carry):
        for j in range(PER):
            for plane, kept, sources in (
                (far, sum_far, [vis_hub]),
                (inner, sum_inner, [vis_hub]),
                (outer, sum_outer, [vis_hub]),
                (y, sum_own, [vis_hub, vis_leaf]),
            ):
                kept[s, j] = partial(tile_of(s, j, plane), mine, sources).astype(kept.dtype)
        return carry

    lax.fori_loop(0, STAGES, first, 0)

    for one in late:
        one.wait()
    for copy in vis_copies[3:]:
        copy.wait_recv()

    def far_copy(s):
        return remote(to_far.at[s], from_far.at[s], nbr_s.at[0, s], nbr_r.at[0, s], inner)

    def inner_copy(s):
        return remote(to_inner.at[s], from_inner.at[s], nbr_s.at[1, s], nbr_r.at[1, s], inner)

    def outer_copy(s):
        return remote(to_outer.at[s], from_outer.at[s], nbr_s.at[2, s], nbr_r.at[2, s], outer)

    def own_copy(s, e, target):
        return pltpu.make_async_remote_copy(
            src_ref=own.at[s, e], dst_ref=target.at[:, chan],
            send_sem=own_s.at[s, e], recv_sem=own_r.at[s, e],
            device_id=(owner(s, e), y), device_id_type=MESH,
        )

    def self_copy(s, target):
        return pltpu.make_async_copy(own.at[s, 0], target.at[:, chan], own_r.at[s, 0])

    def send_own(s, target, last):
        @pl.when(s < last)
        def _():
            own_copy(s, 0, target).start()

        own_copy(s, 1, target).start()

        @pl.when(s == last)
        def _():
            self_copy(last, target).start()

    nchan, width = left.shape[2], left.shape[1]
    slices = nchan // 2 // width

    def lanes_of(q):
        return [pl.multiple_of(side * (nchan // 2) + q * width, width) for side in range(2)]

    def step(it, carry):
        @pl.when(it < STAGES)
        def _():
            s = it
            for j in range(PER):
                to_far[s, j] = (
                    sum_far[s, j].astype(jnp.float32) + partial(tile_of(s, j, far), others, [vis_in])
                ).astype(jnp.bfloat16)
            far_copy(s).start()

        @pl.when((it >= LAG) & (it < STAGES + LAG))
        def _():
            s = it - LAG
            for j in range(PER):
                to_inner[s, j] = (
                    sum_inner[s, j].astype(jnp.float32) + partial(tile_of(s, j, inner), others, [vis_in])
                ).astype(jnp.bfloat16)
            inner_copy(s).start()
            far_copy(s).wait_recv()
            for j in range(PER):
                to_outer[s, j] = (
                    sum_outer[s, j].astype(jnp.float32) + from_far[s, j].astype(jnp.float32)
                ).astype(jnp.bfloat16)
            outer_copy(s).start()

        @pl.when(it >= OWN_LAG)
        def _():
            s = it - OWN_LAG
            gridded = [
                sum_own[s, j, :part_rows].astype(jnp.float32)
                + partial(tile_of(s, j, y), others, [vis_in])
                for j in range(PER)
            ]
            inner_copy(s).wait_recv()
            outer_copy(s).wait_recv()
            for j in range(PER):
                hub_rows = gridded[j] + from_inner[s, j].astype(jnp.float32)
                leaf_rows = sum_own[s, j, part_rows:].astype(jnp.float32) + from_outer[s, j].astype(jnp.float32)
                for lane in range(sums.shape[1]):
                    at = slice(lane * 128, lane * 128 + 128)
                    sums[j, lane, pl.ds(hub_at, part_rows)] = hub_rows[:, at]
                    sums[j, lane, pl.ds(leaf_at, part_rows)] = leaf_rows[:, at]
                for odd in range(2):
                    sorted_rows = [
                        jnp.concatenate(
                            [
                                sums[j, lane, pl.ds(2 * odd + p, part_rows // 2, stride=4)]
                                for p in range(2)
                            ],
                            axis=0,
                        )
                        for lane in range(sums.shape[1])
                    ]
                    own[s, j, odd] = jnp.concatenate(sorted_rows, axis=1).astype(jnp.bfloat16)

            @pl.when(s < half)
            def _():
                send_own(s, grid_first, half - 1)

            @pl.when(s >= half)
            def _():
                send_own(s, grid_out, STAGES - 1)

        @pl.when(it == SLICE_AT)
        def _():
            def received(s, c):
                @pl.when(s < half - 1)
                def _():
                    own_copy(s, 0, grid_first).wait_recv()

                own_copy(s, 1, grid_first).wait_recv()
                return c

            lax.fori_loop(0, half, received, 0)
            self_copy(half - 1, grid_first).wait()

        @pl.when((it >= SLICE_AT) & (it < SLICE_AT + 2))
        def _():
            odd = it - SLICE_AT
            left[odd] = grid_first[odd].reshape(nchan, width).T

        @pl.when((it >= SLICE_AT + 2) & (it < SLICE_AT + 2 + 2 * slices))
        def _():
            c = it - SLICE_AT - 2
            part, q = lax.div(c, slices), lax.rem(c, slices)
            at = pl.multiple_of(part * (nchan // 2) + q * width, width)
            values = delay_slice(
                [left[odd] for odd in range(2)],
                [table[odd, :, pl.ds(at, width)] for odd in range(2)],
            )
            for lane, value in zip(lanes_of(q), values):
                bins = keep[0:1, pl.ds(lane, width)].astype(jnp.float32) * (1.0 / math.sqrt(nchan))
                out[part, :, pl.ds(lane, width)] = value * bins

        return carry

    lax.fori_loop(0, STAGES + OWN_LAG, step, 0)

    for copy in vis_copies:
        copy.wait_send()

    def drain(s, carry):
        for copy in (far_copy(s), inner_copy(s), outer_copy(s)):
            copy.wait_send()

        @pl.when(s < half)
        def _():
            @pl.when(s < half - 1)
            def _():
                own_copy(s, 0, grid_first).wait_send()

            own_copy(s, 1, grid_first).wait_send()

        @pl.when(s >= half)
        def _():
            @pl.when(s < STAGES - 1)
            def _():
                own_copy(s, 0, grid_out).wait()

            own_copy(s, 1, grid_out).wait()

        return carry

    lax.fori_loop(0, STAGES, drain, 0)
    self_copy(STAGES - 1, grid_out).wait()


def delay_slice(left, right):
    even_sum, odd_sum = (
        jnp.dot(one, two, preferred_element_type=jnp.float32) for one, two in zip(left, right)
    )
    return even_sum + odd_sum, even_sum - odd_sum


def delay_kernel(grids, table, keep, first_tile, out_hbm, left, out, sem, first_sem):
    parities, nchan, cells = grids.shape
    half = nchan // 2
    width = cells
    scale = 1.0 / math.sqrt(nchan)
    copies = []
    for part in range(2):
        copy = pltpu.make_async_copy(first_tile.at[part], out_hbm.at[0, part], first_sem.at[part])
        copy.start()
        copies.append(copy)
    turned = [grids[odd].T for odd in range(parities)]
    for part in range(2):
        for q in range(half // width):
            at = part * half + q * width
            values = delay_slice(turned, [table[odd, :, at : at + width] for odd in range(2)])
            for side, value in enumerate(values):
                lane = side * half + q * width
                bins = keep[1:2, lane : lane + width].astype(jnp.float32) * scale
                out[part, :, lane : lane + width] = value * bins
                copy = pltpu.make_async_copy(
                    out.at[part, :, pl.ds(lane, width)],
                    out_hbm.at[1, part, :, pl.ds(lane, width)],
                    sem.at[2 * (part * (half // width) + q) + side],
                )
                copy.start()
                copies.append(copy)
    for copy in copies:
        copy.wait()


def local(n_chan, n_bl, table, visibilities, kernels, block_ids, kernel_ids, tile_counts, wedge_mask):
    blocks, ch_dev = visibilities.shape[:2]
    length, cells = kernels.shape[1:]
    rows = ch_dev * 2
    bf16 = jnp.bfloat16
    part_rows = rows // 2
    stage = (STAGES, PER, part_rows, cells)
    f32 = jnp.float32
    hbm = pl.BlockSpec(memory_space=pltpu.HBM)
    ids = (block_ids.shape[2], block_ids.shape[1])
    operands = (
        block_ids[0].T, kernel_ids[0].T, tile_counts,
        visibilities.reshape(blocks, rows, length), kernels, table, wedge_mask,
    )
    nchan = n_chan * ch_dev
    tiles = wedge_mask.shape[0]
    result = (tiles, 2, cells, nchan)
    grids, first_tile = pl.pallas_call(
        functools.partial(grid_kernel, n_chan, n_bl),
        out_shape=(
            jax.ShapeDtypeStruct((2, n_chan, part_rows, cells), bf16),
            jax.ShapeDtypeStruct(result[1:], f32),
        ),
        in_specs=[hbm] * len(operands),
        out_specs=(pl.BlockSpec(memory_space=pl.ANY), pl.BlockSpec(memory_space=pltpu.VMEM)),
        scratch_shapes=[
            pltpu.SMEM(ids, jnp.int32),
            pltpu.SMEM(ids, jnp.int32),
            pltpu.SMEM(tile_counts.shape, jnp.int32),
            pltpu.VMEM(ids, jnp.int32),
            pltpu.VMEM(ids, jnp.int32),
            pltpu.VMEM(tile_counts.shape, jnp.int32),
            pltpu.SMEM(ids, jnp.int32),
            pltpu.SMEM(ids, jnp.int32),
            pltpu.SMEM(tile_counts.shape, jnp.int32),
            pltpu.VMEM((blocks, part_rows, length), bf16),
            pltpu.VMEM((blocks, part_rows, length), bf16),
            pltpu.VMEM((blocks, part_rows, length), bf16),
            pltpu.VMEM((kernels.shape[0] + 1, length, cells), bf16),
            pltpu.VMEM((PER, cells // 128, rows, 128), f32),
            pltpu.VMEM((STAGES, PER, rows, cells), bf16),
            pltpu.VMEM(stage, bf16),
            pltpu.VMEM(stage, bf16),
            pltpu.VMEM(stage, bf16),
            pltpu.VMEM(stage, bf16),
            pltpu.VMEM(stage, bf16),
            pltpu.VMEM(stage, bf16),
            pltpu.VMEM(stage, bf16),
            pltpu.VMEM(stage, bf16),
            pltpu.VMEM(stage, bf16),
            pltpu.VMEM((STAGES, PER, 2, part_rows, cells), bf16),
            pltpu.VMEM((2, n_chan, part_rows, cells), bf16),
            pltpu.VMEM((2, cells, nchan), bf16),
            pltpu.VMEM(table.shape, bf16),
            pltpu.VMEM(wedge_mask.shape, jnp.int32),
            pltpu.SemaphoreType.DMA((8,)),
            pltpu.SemaphoreType.DMA((7,)),
            pltpu.SemaphoreType.DMA((7,)),
            pltpu.SemaphoreType.DMA((3, STAGES)),
            pltpu.SemaphoreType.DMA((3, STAGES)),
            pltpu.SemaphoreType.DMA((STAGES, 2)),
            pltpu.SemaphoreType.DMA((STAGES, 2)),
        ],
        compiler_params=pltpu.CompilerParams(
            collective_id=0, has_side_effects=True, vmem_limit_bytes=47 << 20
        ),
        name="grid_exchange",
    )(*(pltpu.with_memory_space_constraint(one, pltpu.HBM) for one in operands))
    vmem = pl.BlockSpec(memory_space=pltpu.VMEM)
    return pl.pallas_call(
        delay_kernel,
        out_shape=jax.ShapeDtypeStruct(result, f32),
        in_specs=[vmem, vmem, vmem, vmem],
        out_specs=hbm,
        scratch_shapes=[
            pltpu.VMEM((2, cells, nchan), bf16),
            pltpu.VMEM(result[1:], f32),
            pltpu.SemaphoreType.DMA((2 * nchan // cells,)),
            pltpu.SemaphoreType.DMA((2,)),
        ],
        compiler_params=pltpu.CompilerParams(vmem_limit_bytes=26 << 20),
        cost_estimate=pl.CostEstimate(
            flops=4 * cells * nchan * nchan, bytes_accessed=16 << 20, transcendentals=0
        ),
        name="delay_transform",
    )(
        grids.reshape(2, nchan, cells), table, wedge_mask,
        first_tile,
    )


def solution(mesh):
    def run(visibilities, *rest):
        nchan = visibilities.shape[1]
        table = tables(nchan, nchan // mesh.shape["chan"])
        return jax.shard_map(
            functools.partial(
                local, mesh.shape["chan"], mesh.shape["bl"],
                jnp.asarray(table),
            ),
            mesh=mesh,
            in_specs=(
                P("bl", "chan", None, None),
                P(),
                P("bl", None, None),
                P("bl", None, None),
                P("bl", None),
                P(("chan", "bl"), None),
            ),
            out_specs=P(("chan", "bl"), None, None, None),
            check_vma=False,
        )(visibilities, *rest)

    return run
```

```python
import functools
import math

import jax
import jax.numpy as jnp
import ml_dtypes
import numpy as np
from jax import lax
from jax.experimental import pallas as pl
from jax.experimental.pallas import tpu as pltpu
from jax.sharding import PartitionSpec as P

MESH = pl.DeviceIdType.MESH
STAGES = 32
OFFSETS = (
    (0, 0), (0, 1), (3, 0), (0, 3), (1, 0), (0, 2), (2, 0), (1, 1),
    (3, 3), (1, 3), (3, 1), (2, 1), (1, 2), (2, 3), (3, 2), (2, 2),
)
PER = 2
LAG = 3
OWN_LAG = 7
SLICE_AT = STAGES // 2 + OWN_LAG + 2


def tables(nchan, ch_dev):
    half = nchan // 2
    delays = np.arange(half, dtype=np.int64)
    result = []
    for odd in range(2):
        chans = np.arange(nchan, dtype=np.int64).reshape(nchan // ch_dev, ch_dev)[:, odd::2]
        phase = chans[:, :, None] * delays % nchan
        angle = phase.astype(np.float32) * np.float32(2.0 * math.pi / nchan)
        cosine, sine = np.cos(angle), np.sin(angle)
        real = np.stack([cosine, sine], axis=1)
        imag = np.stack([-sine, cosine], axis=1)
        both = np.concatenate([real, imag], axis=3).reshape(nchan, nchan)
        result.append(both.astype(ml_dtypes.bfloat16))
    return np.stack(result)


def grid_kernel(
    n_chan, n_bl, bid_hbm, kid_hbm, cnt_hbm, vis_hbm, ker_hbm, table_hbm, keep_hbm, grid_out, out,
    bid, kid, cnt, bid_in, kid_in, cnt_in, bid_out, kid_out, cnt_out,
    vis_hub, vis_leaf, vis_in, ker, sums,
    sum_own, sum_inner, sum_far, sum_outer,
    to_inner, to_far, to_outer, from_inner, from_far, from_outer, own,
    grid_first, left, table, keep,
    load_sem, vis_s, vis_r, nbr_s, nbr_r, own_s, own_r,
):
    chan = lax.axis_index("chan")
    y = lax.axis_index("bl")
    core = lax.rem(chan, 2)
    col = lax.rem(lax.div(chan, 2), 4)
    row = lax.div(chan, 8)

    role = lax.rem(y + n_bl - core, n_bl)
    hub = lax.rem(lax.div(role + 1, 2) + 1, 2)
    turn = 2 * lax.rem(role, 2)
    outer = lax.rem(y + 1 + turn, n_bl)
    inner = lax.rem(y + 3 + turn, n_bl)
    far = lax.rem(y + 2, n_bl)

    blocks, part_rows = vis_hub.shape[:2]
    kinds = ker_hbm.shape[0]
    hub_at = pl.multiple_of(hub * part_rows, part_rows)
    leaf_at = pl.multiple_of((1 - hub) * part_rows, part_rows)
    cut = blocks // 4

    barrier = pltpu.get_barrier_semaphore()

    def greet(o, carry):
        pl.semaphore_signal(
            barrier, inc=1, device_id=(lax.rem(chan + o, n_chan), y), device_id_type=MESH
        )
        return carry

    for other in (outer, inner):
        pl.semaphore_signal(barrier, inc=1, device_id=(chan, other), device_id_type=MESH)
    lax.fori_loop(1, n_chan, greet, 0, unroll=True)
    loads = [
        pltpu.make_async_copy(src, dst, load_sem.at[q])
        for q, (src, dst) in enumerate(
            (
                (bid_hbm, bid), (kid_hbm, kid), (cnt_hbm, cnt),
                (ker_hbm, ker.at[pl.ds(0, kinds)]),
                (vis_hbm.at[:, pl.ds(hub_at, part_rows)], vis_hub),
                (vis_hbm.at[:, pl.ds(leaf_at, part_rows)], vis_leaf),
            )
        )
    ]
    for one in loads:
        one.start()
    ker[kinds] = jnp.zeros(ker.shape[1:], ker.dtype)

    pl.semaphore_wait(barrier, n_chan + 1)

    def remote(src, dst, send, recv, plane):
        return pltpu.make_async_remote_copy(
            src_ref=src, dst_ref=dst, send_sem=send, recv_sem=recv,
            device_id=(chan, plane), device_id_type=MESH,
        )

    vis_copies = [
        remote(src, dst, vis_s.at[q], vis_r.at[q], outer)
        for q, (src, dst) in enumerate(
            [(bid_hbm, bid_in), (kid_hbm, kid_in), (cnt_hbm, cnt_in)]
            + [
                (
                    vis_hbm.at[pl.ds(q * cut, cut), pl.ds(leaf_at, part_rows)],
                    vis_in.at[pl.ds(q * cut, cut)],
                )
                for q in range(4)
            ]
        )
    ]
    for copy in vis_copies:
        copy.start()
    for one in loads:
        one.wait()
    late = [
        pltpu.make_async_copy(src, dst, load_sem.at[6 + q])
        for q, (src, dst) in enumerate(((keep_hbm, keep), (table_hbm, table)))
    ]
    for one in late:
        one.start()
    for copy in vis_copies[:3]:
        copy.wait_recv()
    arrived = [
        pltpu.make_async_copy(src, dst, load_sem.at[q])
        for q, (src, dst) in enumerate(((bid_in, bid_out), (kid_in, kid_out), (cnt_in, cnt_out)))
    ]
    for one in arrived:
        one.start()
    for one in arrived:
        one.wait()

    half = STAGES // 2

    def owner(s, e):
        m = half - 1 - lax.rem(s, half)
        dz, dx = 0, 0
        for at, (first_of, second_of) in enumerate(OFFSETS):
            dz = jnp.where(m == at, first_of, dz)
            dx = jnp.where(m == at, second_of, dx)
        return (lax.rem(row + dz, 4) * 4 + lax.rem(col + dx, 4)) * 2 + lax.rem(core + e, 2)

    def tile_of(s, j, plane):
        return (owner(s, j) * n_bl + plane) * 2 + lax.div(s, half)

    def partial(tile, ids, sources):
        block_of, kind_of, count_of = ids
        count = count_of[0, tile]
        left_side, right_side = [], []
        for k in range(8):
            b = block_of[k, tile]
            q = jnp.where(k < count, kind_of[k, tile], kinds)
            chosen = [one[b] for one in sources]
            left_side.append(chosen[0] if len(chosen) == 1 else jnp.concatenate(chosen, axis=0))
            right_side.append(ker[q])
        return jnp.dot(
            jnp.concatenate(left_side, axis=1),
            jnp.concatenate(right_side, axis=0),
            preferred_element_type=jnp.float32,
        )

    mine = (bid, kid, cnt)
    others = (bid_out, kid_out, cnt_out)

    def first(s, carry):
        for j in range(PER):
            for plane, kept, sources in (
                (far, sum_far, [vis_hub]),
                (inner, sum_inner, [vis_hub]),
                (outer, sum_outer, [vis_hub]),
                (y, sum_own, [vis_hub, vis_leaf]),
            ):
                kept[s, j] = partial(tile_of(s, j, plane), mine, sources).astype(kept.dtype)
        return carry

    lax.fori_loop(0, STAGES, first, 0)

    for one in late:
        one.wait()
    for copy in vis_copies[3:]:
        copy.wait_recv()

    def far_copy(s):
        return remote(to_far.at[s], from_far.at[s], nbr_s.at[0, s], nbr_r.at[0, s], inner)

    def inner_copy(s):
        return remote(to_inner.at[s], from_inner.at[s], nbr_s.at[1, s], nbr_r.at[1, s], inner)

    def outer_copy(s):
        return remote(to_outer.at[s], from_outer.at[s], nbr_s.at[2, s], nbr_r.at[2, s], outer)

    def own_copy(s, e, target):
        return pltpu.make_async_remote_copy(
            src_ref=own.at[s, e], dst_ref=target.at[:, chan],
            send_sem=own_s.at[s, e], recv_sem=own_r.at[s, e],
            device_id=(owner(s, e), y), device_id_type=MESH,
        )

    def self_copy(s, target):
        return pltpu.make_async_copy(own.at[s, 0], target.at[:, chan], own_r.at[s, 0])

    def send_own(s, target, last):
        @pl.when(s < last)
        def _():
            own_copy(s, 0, target).start()

        @pl.when(s == last)
        def _():
            self_copy(last, target).start()

    nchan, width = left.shape[2], left.shape[1]
    slices = nchan // 2 // width

    def lanes_of(q):
        return [pl.multiple_of(side * (nchan // 2) + q * width, width) for side in range(2)]

    def step(it, carry):
        @pl.when(it < STAGES)
        def _():
            s = it
            for j in range(PER):
                to_far[s, j] = (
                    sum_far[s, j].astype(jnp.float32) + partial(tile_of(s, j, far), others, [vis_in])
                ).astype(jnp.bfloat16)
            far_copy(s).start()

        @pl.when((it >= LAG) & (it < STAGES + LAG))
        def _():
            s = it - LAG
            for j in range(PER):
                to_inner[s, j] = (
                    sum_inner[s, j].astype(jnp.float32) + partial(tile_of(s, j, inner), others, [vis_in])
                ).astype(jnp.bfloat16)
            inner_copy(s).start()
            far_copy(s).wait_recv()
            for j in range(PER):
                to_outer[s, j] = (
                    sum_outer[s, j].astype(jnp.float32) + from_far[s, j].astype(jnp.float32)
                ).astype(jnp.bfloat16)
            outer_copy(s).start()

        @pl.when(it >= OWN_LAG)
        def _():
            s = it - OWN_LAG
            gridded = [
                sum_own[s, j, :part_rows].astype(jnp.float32)
                + partial(tile_of(s, j, y), others, [vis_in])
                for j in range(PER)
            ]
            inner_copy(s).wait_recv()
            outer_copy(s).wait_recv()
            for j in reversed(range(PER)):
                hub_rows = gridded[j] + from_inner[s, j].astype(jnp.float32)
                leaf_rows = sum_own[s, j, part_rows:].astype(jnp.float32) + from_outer[s, j].astype(jnp.float32)
                for lane in range(sums.shape[1]):
                    at = slice(lane * 128, lane * 128 + 128)
                    sums[j, lane, pl.ds(hub_at, part_rows)] = hub_rows[:, at]
                    sums[j, lane, pl.ds(leaf_at, part_rows)] = leaf_rows[:, at]
                for odd in range(2):
                    sorted_rows = [
                        jnp.concatenate(
                            [
                                sums[j, lane, pl.ds(2 * odd + p, part_rows // 2, stride=4)]
                                for p in range(2)
                            ],
                            axis=0,
                        )
                        for lane in range(sums.shape[1])
                    ]
                    own[s, j, odd] = jnp.concatenate(sorted_rows, axis=1).astype(jnp.bfloat16)

                if j:
                    @pl.when(s < half)
                    def _():
                        own_copy(s, 1, grid_first).start()

                    @pl.when(s >= half)
                    def _():
                        own_copy(s, 1, grid_out).start()

            @pl.when(s < half)
            def _():
                send_own(s, grid_first, half - 1)

            @pl.when(s >= half)
            def _():
                send_own(s, grid_out, STAGES - 1)

        @pl.when(it == SLICE_AT)
        def _():
            def received(s, c):
                @pl.when(s < half - 1)
                def _():
                    own_copy(s, 0, grid_first).wait_recv()

                own_copy(s, 1, grid_first).wait_recv()
                return c

            lax.fori_loop(0, half, received, 0)
            self_copy(half - 1, grid_first).wait()

        @pl.when((it >= SLICE_AT) & (it < SLICE_AT + 2))
        def _():
            odd = it - SLICE_AT
            left[odd] = grid_first[odd].reshape(nchan, width).T

        @pl.when((it >= SLICE_AT + 2) & (it < SLICE_AT + 2 + 2 * slices))
        def _():
            c = it - SLICE_AT - 2
            part, q = lax.div(c, slices), lax.rem(c, slices)
            at = pl.multiple_of(part * (nchan // 2) + q * width, width)
            values = delay_slice(
                [left[odd] for odd in range(2)],
                [table[odd, :, pl.ds(at, width)] for odd in range(2)],
            )
            for lane, value in zip(lanes_of(q), values):
                bins = keep[0:1, pl.ds(lane, width)].astype(jnp.float32) * (1.0 / math.sqrt(nchan))
                out[part, :, pl.ds(lane, width)] = value * bins

        return carry

    lax.fori_loop(0, STAGES + OWN_LAG, step, 0)

    for copy in vis_copies:
        copy.wait_send()

    def drain(s, carry):
        for copy in (far_copy(s), inner_copy(s), outer_copy(s)):
            copy.wait_send()

        @pl.when(s < half)
        def _():
            @pl.when(s < half - 1)
            def _():
                own_copy(s, 0, grid_first).wait_send()

            own_copy(s, 1, grid_first).wait_send()

        @pl.when(s >= half)
        def _():
            @pl.when(s < STAGES - 1)
            def _():
                own_copy(s, 0, grid_out).wait()

            own_copy(s, 1, grid_out).wait()

        return carry

    lax.fori_loop(0, STAGES, drain, 0)
    self_copy(STAGES - 1, grid_out).wait()


def delay_slice(left, right):
    even_sum, odd_sum = (
        jnp.dot(one, two, preferred_element_type=jnp.float32) for one, two in zip(left, right)
    )
    return even_sum + odd_sum, even_sum - odd_sum


def delay_kernel(grids, table, keep, first_tile, out_hbm, left, out, sem, first_sem):
    parities, nchan, cells = grids.shape
    half = nchan // 2
    width = cells
    scale = 1.0 / math.sqrt(nchan)
    copies = []
    for part in range(2):
        copy = pltpu.make_async_copy(first_tile.at[part], out_hbm.at[0, part], first_sem.at[part])
        copy.start()
        copies.append(copy)
    turned = [grids[odd].T for odd in range(parities)]
    for part in range(2):
        for q in range(half // width):
            at = part * half + q * width
            values = delay_slice(turned, [table[odd, :, at : at + width] for odd in range(2)])
            for side, value in enumerate(values):
                lane = side * half + q * width
                bins = keep[1:2, lane : lane + width].astype(jnp.float32) * scale
                out[part, :, lane : lane + width] = value * bins
                copy = pltpu.make_async_copy(
                    out.at[part, :, pl.ds(lane, width)],
                    out_hbm.at[1, part, :, pl.ds(lane, width)],
                    sem.at[2 * (part * (half // width) + q) + side],
                )
                copy.start()
                copies.append(copy)
    for copy in copies:
        copy.wait()


def local(n_chan, n_bl, table, visibilities, kernels, block_ids, kernel_ids, tile_counts, wedge_mask):
    blocks, ch_dev = visibilities.shape[:2]
    length, cells = kernels.shape[1:]
    rows = ch_dev * 2
    bf16 = jnp.bfloat16
    part_rows = rows // 2
    stage = (STAGES, PER, part_rows, cells)
    f32 = jnp.float32
    hbm = pl.BlockSpec(memory_space=pltpu.HBM)
    ids = (block_ids.shape[2], block_ids.shape[1])
    operands = (
        block_ids[0].T, kernel_ids[0].T, tile_counts,
        visibilities.reshape(blocks, rows, length), kernels, table, wedge_mask,
    )
    nchan = n_chan * ch_dev
    tiles = wedge_mask.shape[0]
    result = (tiles, 2, cells, nchan)
    grids, first_tile = pl.pallas_call(
        functools.partial(grid_kernel, n_chan, n_bl),
        out_shape=(
            jax.ShapeDtypeStruct((2, n_chan, part_rows, cells), bf16),
            jax.ShapeDtypeStruct(result[1:], f32),
        ),
        in_specs=[hbm] * len(operands),
        out_specs=(pl.BlockSpec(memory_space=pl.ANY), pl.BlockSpec(memory_space=pltpu.VMEM)),
        scratch_shapes=[
            pltpu.SMEM(ids, jnp.int32),
            pltpu.SMEM(ids, jnp.int32),
            pltpu.SMEM(tile_counts.shape, jnp.int32),
            pltpu.VMEM(ids, jnp.int32),
            pltpu.VMEM(ids, jnp.int32),
            pltpu.VMEM(tile_counts.shape, jnp.int32),
            pltpu.SMEM(ids, jnp.int32),
            pltpu.SMEM(ids, jnp.int32),
            pltpu.SMEM(tile_counts.shape, jnp.int32),
            pltpu.VMEM((blocks, part_rows, length), bf16),
            pltpu.VMEM((blocks, part_rows, length), bf16),
            pltpu.VMEM((blocks, part_rows, length), bf16),
            pltpu.VMEM((kernels.shape[0] + 1, length, cells), bf16),
            pltpu.VMEM((PER, cells // 128, rows, 128), f32),
            pltpu.VMEM((STAGES, PER, rows, cells), bf16),
            pltpu.VMEM(stage, bf16),
            pltpu.VMEM(stage, bf16),
            pltpu.VMEM(stage, bf16),
            pltpu.VMEM(stage, bf16),
            pltpu.VMEM(stage, bf16),
            pltpu.VMEM(stage, bf16),
            pltpu.VMEM(stage, bf16),
            pltpu.VMEM(stage, bf16),
            pltpu.VMEM(stage, bf16),
            pltpu.VMEM((STAGES, PER, 2, part_rows, cells), bf16),
            pltpu.VMEM((2, n_chan, part_rows, cells), bf16),
            pltpu.VMEM((2, cells, nchan), bf16),
            pltpu.VMEM(table.shape, bf16),
            pltpu.VMEM(wedge_mask.shape, jnp.int32),
            pltpu.SemaphoreType.DMA((8,)),
            pltpu.SemaphoreType.DMA((7,)),
            pltpu.SemaphoreType.DMA((7,)),
            pltpu.SemaphoreType.DMA((3, STAGES)),
            pltpu.SemaphoreType.DMA((3, STAGES)),
            pltpu.SemaphoreType.DMA((STAGES, 2)),
            pltpu.SemaphoreType.DMA((STAGES, 2)),
        ],
        compiler_params=pltpu.CompilerParams(
            collective_id=0, has_side_effects=True, vmem_limit_bytes=47 << 20
        ),
        name="grid_exchange",
    )(*(pltpu.with_memory_space_constraint(one, pltpu.HBM) for one in operands))
    vmem = pl.BlockSpec(memory_space=pltpu.VMEM)
    return pl.pallas_call(
        delay_kernel,
        out_shape=jax.ShapeDtypeStruct(result, f32),
        in_specs=[vmem, vmem, vmem, vmem],
        out_specs=hbm,
        scratch_shapes=[
            pltpu.VMEM((2, cells, nchan), bf16),
            pltpu.VMEM(result[1:], f32),
            pltpu.SemaphoreType.DMA((2 * nchan // cells,)),
            pltpu.SemaphoreType.DMA((2,)),
        ],
        compiler_params=pltpu.CompilerParams(vmem_limit_bytes=26 << 20),
        cost_estimate=pl.CostEstimate(
            flops=4 * cells * nchan * nchan, bytes_accessed=16 << 20, transcendentals=0
        ),
        name="delay_transform",
    )(
        grids.reshape(2, nchan, cells), table, wedge_mask,
        first_tile,
    )


def solution(mesh):
    def run(visibilities, *rest):
        nchan = visibilities.shape[1]
        table = tables(nchan, nchan // mesh.shape["chan"])
        return jax.shard_map(
            functools.partial(
                local, mesh.shape["chan"], mesh.shape["bl"],
                jnp.asarray(table),
            ),
            mesh=mesh,
            in_specs=(
                P("bl", "chan", None, None),
                P(),
                P("bl", None, None),
                P("bl", None, None),
                P("bl", None),
                P(("chan", "bl"), None),
            ),
            out_specs=P(("chan", "bl"), None, None, None),
            check_vma=False,
        )(visibilities, *rest)

    return run
```
